256 devices in a mesh: px: 16 (over z, y_hi), py: 16 (over x, y_lo, core).
Axes of the slice: x: 4, y: 4 (y_hi: 2, y_lo: 2; y = y_hi * 2 + y_lo), z: 8, core: 2. Of those that a mesh axis runs over, the one named last changes fastest.
Arguments:
- estimate: float32 [512, 512, 128], P('px', 'py'), may hold values from 0.2 to 5
- observed: float32 [512, 512, 128], P('px', 'py'), may hold values from 0.2 to 5
- psf: float32 [32, 32, 32], replicated, as said below
Outputs:
- updated: float32 [512, 512, 128], P('px', 'py')
The draws below stay inside these ranges and needn't reach their ends.
Inputs may be any that keep to these rules, and one draw needn't show every extreme that they name: `psf`: every entry is positive.
All inputs are finite; a program needn't handle non-finite values.
Results may differ from the reference program's by a relative error of at most 0.00009.
Values sent between devices are 32-bit elements; how exact they have to be, the bound alone decides.
No kernel may reach another device: no remote copies, remote signals or barrier semaphores. Data moves between devices by JAX's collectives and lax.ppermute only.
A program may use at most 128 MiB of HBM per device.

```python
import math
import jax
import jax.numpy as jnp
from jax import lax

NX = 512
NY = 512
NZ = 128
P_SIZE = 32


def draw_psf(key, part):
    offsets = (jnp.arange(P_SIZE) - P_SIZE // 2).astype(jnp.float32)
    lateral = offsets[:, None, None] * offsets[:, None, None] + offsets[None, :, None] * offsets[None, :, None]
    axial = offsets[None, None, :] * offsets[None, None, :]
    radius = jnp.sqrt(lateral / 4.0 + axial / 16.0)
    factor = jnp.exp(jax.random.uniform(key, (P_SIZE, P_SIZE, P_SIZE), jnp.float32, math.log(0.5), math.log(2.0)))
    return factor * jnp.exp(-radius)


def levels(rng, dims, cuts, low, top_value):
    factor_of, own = 1.0, jax.random.fold_in(rng, 6)
    for dim, parts in cuts:
        draws = jnp.exp(jax.random.uniform(jax.random.fold_in(own, dim), (parts,), jnp.float32, low / len(cuts), top_value / len(cuts)))
        factor_of = factor_of * jnp.repeat(draws, dims[dim] // parts).reshape([-1 if axis == dim else 1 for axis in range(len(dims))])
    return factor_of


def setup_inputs(seed: int = 0) -> dict:
    key_of = jax.random.split(jax.random.key(seed), 4)
    return {
        "estimate": jnp.clip(jnp.exp(math.log(5.0) - 3.218876 * jax.random.uniform(key_of[0], (NX, NY, NZ), jnp.float32) ** levels(key_of[0], (NX, NY, NZ), ((0, 16), (1, 16)), -0.2, 0.2)), 0.2, 5.0),
        "observed": jnp.clip(jnp.exp(math.log(5.0) - 3.218876 * jax.random.uniform(key_of[1], (NX, NY, NZ), jnp.float32) ** levels(key_of[1], (NX, NY, NZ), ((0, 16), (1, 16)), -0.2, 0.2)), 0.2, 5.0),
        "psf": draw_psf(jax.random.fold_in(key_of[3], 71), 0),
    }


penalty_weight = 0.1
smoothing = 0.1

def backward_rows(flux):
    return flux - jnp.concatenate([jnp.zeros_like(flux[:1]), flux[:-1]], 0)

def backward_columns(flux):
    return flux - jnp.concatenate([jnp.zeros_like(flux[:, :1]), flux[:, :-1]], 1)

def backward_depth(flux):
    return flux - jnp.concatenate([jnp.zeros_like(flux[:, :, :1]), flux[:, :, :-1]], 2)

def variation(volume):
    slope_rows = jnp.concatenate([volume[1:] - volume[:-1], jnp.zeros_like(volume[:1])], 0)
    slope_cols = jnp.concatenate([volume[:, 1:] - volume[:, :-1], jnp.zeros_like(volume[:, :1])], 1)
    slope_depth = jnp.concatenate([volume[:, :, 1:] - volume[:, :, :-1], jnp.zeros_like(volume[:, :, :1])], 2)
    factor = lax.rsqrt(slope_rows * slope_rows + slope_cols * slope_cols + slope_depth * slope_depth + smoothing * smoothing)
    return backward_rows(slope_rows * factor) + backward_columns(slope_cols * factor) + backward_depth(slope_depth * factor)

def reference(estimate, observed, psf):
    padded = jnp.zeros((NX, NY, NZ), jnp.float32).at[:P_SIZE, :P_SIZE, :P_SIZE].set(psf)
    padded = jnp.roll(padded, (-(P_SIZE // 2), -(P_SIZE // 2), -(P_SIZE // 2)), axis=(0, 1, 2))
    transfer = jnp.fft.fftn(padded)
    blurred = jnp.real(jnp.fft.ifftn(jnp.fft.fftn(estimate) * transfer)).astype(jnp.float32)
    quotient = observed / blurred
    correction = jnp.real(jnp.fft.ifftn(jnp.fft.fftn(quotient) * jnp.conj(transfer))).astype(jnp.float32)
    divergence = variation(estimate)
    return estimate * correction / (1.0 - penalty_weight * divergence)
```

```python
import functools
import math

import jax
import jax.numpy as jnp
import ml_dtypes
import numpy as np
from jax import lax
from jax.experimental import pallas as pl
from jax.experimental.pallas import tpu as pltpu
from jax.sharding import PartitionSpec as P

penalty_weight = 0.1
smoothing = 0.1

WINDOW = 64
PLANES = 34
ROOT = math.sqrt(0.5)


def two_part(matrix):
    high = matrix.astype(ml_dtypes.bfloat16)
    low = (matrix - high.astype(np.float64)).astype(ml_dtypes.bfloat16)
    return high, low


def right_operand(matrix):
    high, low = two_part(matrix)
    return np.block([[high, low], [high, np.zeros_like(high)]])


def left_operand(matrix):
    high, low = two_part(matrix)
    return np.block([[high, high], [low, np.zeros_like(high)]])


def depth_forward(positions, depth):
    half = depth // 2
    turns = 2.0 * np.pi / depth
    real = np.cos(turns * np.outer(positions, np.arange(half + 1)))
    imag = -np.sin(turns * np.outer(positions, np.arange(1, half)))
    return np.concatenate([real, imag], 1)


def depth_inverse(depth):
    half = depth // 2
    turns = 2.0 * np.pi / depth
    positions = np.arange(depth)
    weight = np.full(half + 1, 2.0)
    weight[0] = weight[half] = 1.0
    real = weight[:, None] * np.cos(turns * np.outer(np.arange(half + 1), positions))
    imag = -2.0 * np.sin(turns * np.outer(np.arange(1, half), positions))
    return np.concatenate([real, imag], 0)


def column_forward(positions):
    angles = 2.0 * np.pi / WINDOW * np.outer(np.arange(WINDOW), positions)
    cosine, sine = np.cos(angles), np.sin(angles)
    return np.block([[cosine, sine], [-sine, cosine]])


def column_inverse(positions):
    angles = 2.0 * np.pi / WINDOW * np.outer(positions, np.arange(WINDOW))
    cosine, sine = np.cos(angles), np.sin(angles)
    return np.block([[cosine, -sine], [sine, cosine]])


def add(a, b):
    return (a[0] + b[0], a[1] + b[1])


def sub(a, b):
    return (a[0] - b[0], a[1] - b[1])


def turn(a, eighths):
    real, imag = a
    eighths %= 8
    if eighths == 0:
        return a
    if eighths == 2:
        return (-imag, real)
    if eighths == 4:
        return (-real, -imag)
    if eighths == 6:
        return (imag, -real)
    total, gap = (real + imag) * ROOT, (real - imag) * ROOT
    if eighths == 1:
        return (gap, total)
    if eighths == 3:
        return (-total, gap)
    if eighths == 5:
        return (-gap, -total)
    return (total, -gap)


def twiddle(a, power, sign):
    angle = sign * 2.0 * math.pi * power / WINDOW
    cosine, sine = math.cos(angle), math.sin(angle)
    if power == 0:
        return a
    real, imag = a
    return (real * cosine - imag * sine, real * sine + imag * cosine)


def complex_eight(values, sign):
    if len(values) == 1:
        return values
    count = len(values)
    even = complex_eight(values[0::2], sign)
    odd = complex_eight(values[1::2], sign)
    odd = [turn(value, sign * k * (8 // count)) for k, value in enumerate(odd)]
    return [add(e, o) for e, o in zip(even, odd)] + [sub(e, o) for e, o in zip(even, odd)]


def real_eight(a):
    s04, d04, s26, d26 = a[0] + a[4], a[0] - a[4], a[2] + a[6], a[2] - a[6]
    s15, d15, s37, d37 = a[1] + a[5], a[1] - a[5], a[3] + a[7], a[3] - a[7]
    even, odd = s04 + s26, s15 + s37
    gap, total = (d15 - d37) * ROOT, (d15 + d37) * ROOT
    return (
        even + odd,
        (d04 + gap, -d26 - total),
        (s04 - s26, s37 - s15),
        (d04 - gap, d26 - total),
        even - odd,
    )


def rows_forward(load, store, zero):
    first = [real_eight([load(8 * x1 + x0) for x1 in range(8)]) for x0 in range(8)]
    ends = real_eight([f[0] for f in first])
    store(0, ends[0], zero)
    for k0 in (1, 2, 3):
        store(k0, *ends[k0])
    store(4, ends[4], zero)
    plane = 5
    for k1 in (1, 2, 3):
        out = complex_eight([twiddle(first[x0][k1], k1 * x0, -1) for x0 in range(8)], -1)
        for value in out:
            store(plane, *value)
            plane += 1
    middle = []
    for x0 in range(8):
        angle = 2.0 * math.pi * 4 * x0 / WINDOW
        middle.append((first[x0][4] * math.cos(angle), first[x0][4] * -math.sin(angle)))
    middle = complex_eight(middle, -1)
    for k0 in range(4):
        store(plane, *middle[k0])
        plane += 1


def rows_inverse(load, store):
    ends = [load(p) for p in range(5)]
    x0r, x4r = ends[0][0], ends[4][0]
    spectrum = [(x0r, jnp.zeros_like(x0r))] + [ends[k] for k in (1, 2, 3)]
    parts = [[None] * 8 for _ in range(5)]
    (r1, i1), (r2, i2), (r3, i3) = [(2.0 * e[0], 2.0 * e[1]) for e in ends[1:4]]
    del spectrum
    base, flip = x0r + x4r, x0r - x4r
    g13, t13 = r1 - r3, r1 + r3
    h13, u13 = i1 - i3, i1 + i3
    parts[0][0] = base + t13 + r2
    parts[0][4] = base - t13 + r2
    parts[0][2] = base - r2 - h13
    parts[0][6] = base - r2 + h13
    odd_a, odd_b = g13 * ROOT, u13 * ROOT
    parts[0][1] = flip + odd_a - odd_b - i2
    parts[0][5] = flip - odd_a + odd_b - i2
    parts[0][3] = flip - odd_a - odd_b + i2
    parts[0][7] = flip + odd_a + odd_b + i2
    plane = 5
    for k1 in (1, 2, 3):
        values = complex_eight([load(plane + k0) for k0 in range(8)], 1)
        plane += 8
        parts[k1] = [twiddle(values[x0], k1 * x0, 1) for x0 in range(8)]
    half = [load(plane + k0) for k0 in range(4)]
    middle = complex_eight(half + [(half[3 - k][0], -half[3 - k][1]) for k in range(4)], 1)
    for x0 in range(8):
        angle = 2.0 * math.pi * 4 * x0 / WINDOW
        parts[4][x0] = middle[x0][0] * math.cos(angle) - middle[x0][1] * math.sin(angle)
    for x0 in range(8):
        v0, v4 = parts[0][x0], parts[4][x0]
        (a, b), (c, d), (e, f) = parts[1][x0], parts[2][x0], parts[3][x0]
        plus, minus = v0 + v4, v0 - v4
        store(16 + x0, plus + 2.0 * (f - b - c))
        store(24 + x0, minus + 2.0 * (d + ROOT * ((e - f) - (a + b))))
        store(32 + x0, plus + 2.0 * (c - a - e))
        store(40 + x0, minus + 2.0 * (ROOT * ((b - a) + (e + f)) - d))


def parts_of(value):
    high = value.astype(jnp.bfloat16)
    low = (value - high.astype(jnp.float32)).astype(jnp.bfloat16)
    return high, low


def along_depth(rows, matrix):
    high, low = parts_of(rows)
    out = jnp.dot(
        jnp.concatenate([high, low], 1), matrix, preferred_element_type=jnp.float32
    )
    return out[:, :128] + out[:, 128:]


def along_columns(matrix, value):
    high, low = parts_of(value)
    out = jnp.dot(
        matrix, jnp.concatenate([high, low], 0), preferred_element_type=jnp.float32
    )
    half = out.shape[0] // 2
    return out[:half] + out[half:]


def transfer_kernel(psf_ref, depth_ref, column_ref, out_ref, field, rows):
    size = psf_ref.shape[0]
    for x in range(0, size, 8):
        values = psf_ref[x : x + 8].reshape(8 * size, size)
        field[x : x + 8] = jnp.dot(
            values,
            depth_ref[...],
            precision=lax.Precision.HIGHEST,
            preferred_element_type=jnp.float32,
        ).reshape(8, size, 128)
    zero = jnp.zeros((8, 128), jnp.float32)

    def chunk(c, carry):
        here = pl.ds(pl.multiple_of(c * 8, 8), 8)
        there = pl.ds(pl.multiple_of(c * 8 + size, 8), 8)

        def load(x):
            tap = (x + size // 2) % WINDOW
            return field[tap, here, :] if tap < size else zero

        def store(plane, real, imag):
            rows[plane, here, :] = real
            rows[plane, there, :] = imag

        rows_forward(load, store, zero)
        return carry

    lax.fori_loop(0, size // 8, chunk, 0)
    lane = lax.broadcasted_iota(jnp.int32, (1, 128), 1)
    real_lane = lane <= 64
    first_half = lane < 64
    alone = (lane == 0) | (lane == 64)

    def plane_of(p, carry):
        spectrum = jnp.dot(
            column_ref[...],
            rows[p],
            precision=lax.Precision.HIGHEST,
            preferred_element_type=jnp.float32,
        )
        other = pltpu.roll(spectrum, 64, 1)
        own = jnp.where(real_lane, spectrum, other)
        partner = jnp.where(alone, 0.0, jnp.where(first_half, -other, spectrum))
        out_ref[p, :128, :] = own
        out_ref[p, 128:, :] = partner
        return carry

    lax.fori_loop(0, PLANES - 1, plane_of, 0)
    out_ref[PLANES - 1] = jnp.zeros_like(out_ref[0])


def convolve_kernel(
    adjoint,
    own_ref,
    top_ref,
    bottom_ref,
    left_ref,
    right_ref,
    transfer_ref,
    other_ref,
    depth_ref,
    column_ref,
    column_back_ref,
    depth_back_ref,
    out_ref,
    field,
    rows,
    back,
):
    depth_matrix = depth_ref[...]

    def depth_piece(ref, x_from, y_from, step):
        count, width, lanes = ref.shape
        for x in range(0, count, step):
            values = ref[x : x + step].reshape(step * width, lanes)
            field[x_from + x : x_from + x + step, y_from : y_from + width, :] = along_depth(
                values, depth_matrix
            ).reshape(step, width, lanes)

    depth_piece(own_ref, 16, 16, 8)
    depth_piece(top_ref, 0, 16, 8)
    depth_piece(bottom_ref, 48, 16, 8)
    depth_piece(left_ref, 0, 0, 16)
    depth_piece(right_ref, 0, 48, 16)

    zero = jnp.zeros((8, 128), jnp.float32)
    rows[PLANES - 1] = jnp.zeros_like(rows[0])

    def chunk(c, carry):
        here = pl.ds(pl.multiple_of(c * 8, 8), 8)
        there = pl.ds(pl.multiple_of(c * 8 + WINDOW, 8), 8)

        def load(x):
            return field[x, here, :]

        def store(plane, real, imag):
            rows[plane, here, :] = real
            rows[plane, there, :] = imag

        rows_forward(load, store, zero)
        return carry

    lax.fori_loop(0, WINDOW // 8, chunk, 0)

    def pair(i, carry):
        p = i * 2
        spectrum = along_columns(
            column_ref[...], jnp.concatenate([rows[p], rows[p + 1]], 1)
        )
        weighted = []
        for k in range(2):
            own = spectrum[:, 128 * k : 128 * (k + 1)]
            partner = pltpu.roll(own, 64, 1)
            a, b = own[:64], own[64:]
            c, d = partner[:64], partner[64:]
            fr, fi = transfer_ref[p + k, 0:64, :], transfer_ref[p + k, 64:128, :]
            gr, gi = transfer_ref[p + k, 128:192, :], transfer_ref[p + k, 192:256, :]
            if adjoint:
                real = (a * fr + b * fi) - (c * gr + d * gi)
                imag = (b * fr - a * fi) - (d * gr - c * gi)
            else:
                real = (a * fr - b * fi) + (c * gr - d * gi)
                imag = (b * fr + a * fi) + (d * gr + c * gi)
            weighted.append(jnp.concatenate([real, imag], 0))
        result = along_columns(column_back_ref[...], jnp.concatenate(weighted, 1))
        back[p] = result[:, :128]
        back[p + 1] = result[:, 128:]
        return carry

    lax.fori_loop(0, PLANES // 2, pair, 0, unroll=PLANES // 2)

    def chunk_back(c, carry):
        here = pl.ds(pl.multiple_of(c * 8, 8), 8)
        there = pl.ds(pl.multiple_of(c * 8 + 32, 8), 8)

        def load(plane):
            return back[plane, here, :], back[plane, there, :]

        def store(x, value):
            field[x, here, :] = value

        rows_inverse(load, store)
        return carry

    lax.fori_loop(0, 4, chunk_back, 0)

    matrix = depth_back_ref[...]
    for x in range(0, 32, 8):
        values = field[16 + x : 24 + x, 0:32, :].reshape(256, 128)
        result = along_depth(values, matrix).reshape(8, 32, 128)
        if adjoint:
            out_ref[x : x + 8] = other_ref[x : x + 8] * result
        else:
            out_ref[x : x + 8] = other_ref[x : x + 8] / result


def vmem(count):
    return [pl.BlockSpec(memory_space=pltpu.VMEM)] * count


def transfer_function(psf, depth):
    size = psf.shape[0]
    offsets = np.arange(size) - size // 2
    return pl.pallas_call(
        transfer_kernel,
        out_shape=jax.ShapeDtypeStruct((PLANES, 256, 128), jnp.float32),
        in_specs=vmem(3),
        out_specs=pl.BlockSpec(memory_space=pltpu.VMEM),
        scratch_shapes=[
            pltpu.VMEM((size, size, 128), jnp.float32),
            pltpu.VMEM((PLANES - 1, 2 * size, 128), jnp.float32),
        ],
        compiler_params=pltpu.CompilerParams(vmem_limit_bytes=32 * 2**20),
        name="transfer",
    )(
        psf,
        jnp.asarray(depth_forward(offsets, depth), jnp.float32),
        jnp.asarray(column_forward(offsets), jnp.float32),
    )


def convolve(pieces, transfer, other, adjoint):
    depth = other.shape[2]
    positions = np.arange(WINDOW)
    scale = 1.0 / (WINDOW * WINDOW * depth)
    return pl.pallas_call(
        functools.partial(convolve_kernel, adjoint),
        out_shape=jax.ShapeDtypeStruct(other.shape, jnp.float32),
        in_specs=vmem(11),
        out_specs=pl.BlockSpec(memory_space=pltpu.VMEM),
        scratch_shapes=[
            pltpu.VMEM((WINDOW, WINDOW, depth), jnp.float32),
            pltpu.VMEM((PLANES, 2 * WINDOW, depth), jnp.float32),
            pltpu.VMEM((PLANES, WINDOW, depth), jnp.float32),
        ],
        compiler_params=pltpu.CompilerParams(vmem_limit_bytes=48 * 2**20),
        name="correlate" if adjoint else "convolve",
    )(
        *pieces,
        transfer,
        other,
        right_operand(depth_forward(np.arange(depth), depth)),
        left_operand(column_forward(positions)),
        left_operand(column_inverse(positions[16:48])),
        right_operand(depth_inverse(depth) * scale),
    )


def halos(block):
    def ring(axis, step):
        count = lax.axis_size(axis)
        return [(i, (i + step) % count) for i in range(count)]

    top = lax.ppermute(block[16:], "px", ring("px", 1))
    bottom = lax.ppermute(block[:16], "px", ring("px", -1))
    ends = jnp.concatenate([top[:, 16:], block[:, 16:], bottom[:, 16:]], 0)
    starts = jnp.concatenate([top[:, :16], block[:, :16], bottom[:, :16]], 0)
    left = lax.ppermute(ends, "py", ring("py", 1))
    right = lax.ppermute(starts, "py", ring("py", -1))
    return block, top, bottom, left, right


def variation(pieces):
    volume, top, bottom, left, right = pieces
    row_count, col_count, _ = volume.shape
    row_whole = row_count * lax.axis_size("px")
    col_whole = col_count * lax.axis_size("py")
    padded = jnp.concatenate(
        [
            left[15:49, 15:],
            jnp.concatenate([top[15:], volume, bottom[:1]], 0),
            right[15:49, :1],
        ],
        1,
    )
    region = padded[:-1, :-1]
    slope_rows = padded[1:, :-1] - region
    slope_cols = padded[:-1, 1:] - region
    row_global = lax.axis_index("px") * row_count - 1 + jnp.arange(row_count + 1)
    col_global = lax.axis_index("py") * col_count - 1 + jnp.arange(col_count + 1)
    row_valid = ((row_global >= 0) & (row_global <= row_whole - 2))[:, None, None]
    col_valid = ((col_global >= 0) & (col_global <= col_whole - 2))[None, :, None]
    slope_rows = jnp.where(row_valid, slope_rows, 0.0)
    slope_cols = jnp.where(col_valid, slope_cols, 0.0)
    slope_depth = jnp.concatenate(
        [region[:, :, 1:] - region[:, :, :-1], jnp.zeros_like(region[:, :, :1])], 2
    )
    factor = lax.rsqrt(
        slope_rows * slope_rows
        + slope_cols * slope_cols
        + slope_depth * slope_depth
        + smoothing * smoothing
    )
    flux_rows, flux_cols = slope_rows * factor, slope_cols * factor
    flux_depth = (slope_depth * factor)[1:, 1:]
    flux_depth = flux_depth - jnp.concatenate(
        [jnp.zeros_like(flux_depth[:, :, :1]), flux_depth[:, :, :-1]], 2
    )
    return (
        flux_rows[1:, 1:]
        - flux_rows[:-1, 1:]
        + (flux_cols[1:, 1:] - flux_cols[1:, :-1])
        + flux_depth
    )


def shards(estimate, observed, psf):
    transfer = transfer_function(psf, estimate.shape[2])
    pieces = halos(estimate)
    quotient = convolve(pieces, transfer, observed, False)
    scaled = estimate / (1.0 - penalty_weight * variation(pieces))
    return convolve(halos(quotient), transfer, scaled, True)


def solution(mesh):
    placed = (P("px", "py", None), P("px", "py", None), P())
    return jax.shard_map(
        shards, mesh=mesh, in_specs=placed, out_specs=P("px", "py", None), check_vma=False
    )
```

```python
import functools
import math

import jax
import jax.numpy as jnp
import ml_dtypes
import numpy as np
from jax import lax
from jax.experimental import pallas as pl
from jax.experimental.pallas import tpu as pltpu
from jax.sharding import PartitionSpec as P

penalty_weight = 0.1
smoothing = 0.1

WINDOW = 64
PLANES = 34
ROOT = math.sqrt(0.5)


def two_part(matrix):
    high = matrix.astype(ml_dtypes.bfloat16)
    low = (matrix - high.astype(np.float64)).astype(ml_dtypes.bfloat16)
    return high, low


def right_operand(matrix):
    high, low = two_part(matrix)
    return np.block([[high, low], [high, np.zeros_like(high)]])


def left_operand(matrix):
    high, low = two_part(matrix)
    return np.block([[high, high], [low, np.zeros_like(high)]])


def depth_forward(positions, depth):
    half = depth // 2
    turns = 2.0 * np.pi / depth
    real = np.cos(turns * np.outer(positions, np.arange(half + 1)))
    imag = -np.sin(turns * np.outer(positions, np.arange(1, half)))
    return np.concatenate([real, imag], 1)


def depth_inverse(depth):
    half = depth // 2
    turns = 2.0 * np.pi / depth
    positions = np.arange(depth)
    weight = np.full(half + 1, 2.0)
    weight[0] = weight[half] = 1.0
    real = weight[:, None] * np.cos(turns * np.outer(np.arange(half + 1), positions))
    imag = -2.0 * np.sin(turns * np.outer(np.arange(1, half), positions))
    return np.concatenate([real, imag], 0)


def column_forward(positions):
    angles = 2.0 * np.pi / WINDOW * np.outer(np.arange(WINDOW), positions)
    cosine, sine = np.cos(angles), np.sin(angles)
    return np.block([[cosine, sine], [-sine, cosine]])


def column_inverse(positions):
    angles = 2.0 * np.pi / WINDOW * np.outer(positions, np.arange(WINDOW))
    cosine, sine = np.cos(angles), np.sin(angles)
    return np.block([[cosine, -sine], [sine, cosine]])


def add(a, b):
    return (a[0] + b[0], a[1] + b[1])


def sub(a, b):
    return (a[0] - b[0], a[1] - b[1])


def turn(a, eighths):
    real, imag = a
    eighths %= 8
    if eighths == 0:
        return a
    if eighths == 2:
        return (-imag, real)
    if eighths == 4:
        return (-real, -imag)
    if eighths == 6:
        return (imag, -real)
    total, gap = (real + imag) * ROOT, (real - imag) * ROOT
    if eighths == 1:
        return (gap, total)
    if eighths == 3:
        return (-total, gap)
    if eighths == 5:
        return (-gap, -total)
    return (total, -gap)


def twiddle(a, power, sign):
    angle = sign * 2.0 * math.pi * power / WINDOW
    cosine, sine = math.cos(angle), math.sin(angle)
    if power == 0:
        return a
    real, imag = a
    return (real * cosine - imag * sine, real * sine + imag * cosine)


def complex_eight(values, sign):
    if len(values) == 1:
        return values
    count = len(values)
    even = complex_eight(values[0::2], sign)
    odd = complex_eight(values[1::2], sign)
    odd = [turn(value, sign * k * (8 // count)) for k, value in enumerate(odd)]
    return [add(e, o) for e, o in zip(even, odd)] + [sub(e, o) for e, o in zip(even, odd)]


def real_eight(a):
    s04, d04, s26, d26 = a[0] + a[4], a[0] - a[4], a[2] + a[6], a[2] - a[6]
    s15, d15, s37, d37 = a[1] + a[5], a[1] - a[5], a[3] + a[7], a[3] - a[7]
    even, odd = s04 + s26, s15 + s37
    gap, total = (d15 - d37) * ROOT, (d15 + d37) * ROOT
    return (
        even + odd,
        (d04 + gap, -d26 - total),
        (s04 - s26, s37 - s15),
        (d04 - gap, d26 - total),
        even - odd,
    )


def rows_forward(load, store, zero):
    first = [real_eight([load(8 * x1 + x0) for x1 in range(8)]) for x0 in range(8)]
    ends = real_eight([f[0] for f in first])
    store(0, ends[0], zero)
    for k0 in (1, 2, 3):
        store(k0, *ends[k0])
    store(4, ends[4], zero)
    plane = 5
    for k1 in (1, 2, 3):
        out = complex_eight([twiddle(first[x0][k1], k1 * x0, -1) for x0 in range(8)], -1)
        for value in out:
            store(plane, *value)
            plane += 1
    middle = []
    for x0 in range(8):
        angle = 2.0 * math.pi * 4 * x0 / WINDOW
        middle.append((first[x0][4] * math.cos(angle), first[x0][4] * -math.sin(angle)))
    middle = complex_eight(middle, -1)
    for k0 in range(4):
        store(plane, *middle[k0])
        plane += 1


def rows_inverse(load, store):
    ends = [load(p) for p in range(5)]
    x0r, x4r = ends[0][0], ends[4][0]
    spectrum = [(x0r, jnp.zeros_like(x0r))] + [ends[k] for k in (1, 2, 3)]
    parts = [[None] * 8 for _ in range(5)]
    (r1, i1), (r2, i2), (r3, i3) = [(2.0 * e[0], 2.0 * e[1]) for e in ends[1:4]]
    del spectrum
    base, flip = x0r + x4r, x0r - x4r
    g13, t13 = r1 - r3, r1 + r3
    h13, u13 = i1 - i3, i1 + i3
    parts[0][0] = base + t13 + r2
    parts[0][4] = base - t13 + r2
    parts[0][2] = base - r2 - h13
    parts[0][6] = base - r2 + h13
    odd_a, odd_b = g13 * ROOT, u13 * ROOT
    parts[0][1] = flip + odd_a - odd_b - i2
    parts[0][5] = flip - odd_a + odd_b - i2
    parts[0][3] = flip - odd_a - odd_b + i2
    parts[0][7] = flip + odd_a + odd_b + i2
    plane = 5
    for k1 in (1, 2, 3):
        values = complex_eight([load(plane + k0) for k0 in range(8)], 1)
        plane += 8
        parts[k1] = [twiddle(values[x0], k1 * x0, 1) for x0 in range(8)]
    half = [load(plane + k0) for k0 in range(4)]
    middle = complex_eight(half + [(half[3 - k][0], -half[3 - k][1]) for k in range(4)], 1)
    for x0 in range(8):
        angle = 2.0 * math.pi * 4 * x0 / WINDOW
        parts[4][x0] = middle[x0][0] * math.cos(angle) - middle[x0][1] * math.sin(angle)
    for x0 in range(8):
        v0, v4 = parts[0][x0], parts[4][x0]
        (a, b), (c, d), (e, f) = parts[1][x0], parts[2][x0], parts[3][x0]
        plus, minus = v0 + v4, v0 - v4
        store(16 + x0, plus + 2.0 * (f - b - c))
        store(24 + x0, minus + 2.0 * (d + ROOT * ((e - f) - (a + b))))
        store(32 + x0, plus + 2.0 * (c - a - e))
        store(40 + x0, minus + 2.0 * (ROOT * ((b - a) + (e + f)) - d))


def parts_of(value):
    high = value.astype(jnp.bfloat16)
    low = (value - high.astype(jnp.float32)).astype(jnp.bfloat16)
    return high, low


def along_depth(rows, matrix):
    high, low = parts_of(rows)
    out = jnp.dot(
        jnp.concatenate([high, low], 1), matrix, preferred_element_type=jnp.float32
    )
    return out[:, :128] + out[:, 128:]


def along_columns(matrix, value):
    high, low = parts_of(value)
    out = jnp.dot(
        matrix, jnp.concatenate([high, low], 0), preferred_element_type=jnp.float32
    )
    half = out.shape[0] // 2
    return out[:half] + out[half:]


def transfer_kernel(psf_ref, depth_ref, column_ref, out_ref, field, rows, factors, done):
    size = psf_ref.shape[0]
    for x in range(0, size, 8):
        values = psf_ref[x : x + 8].reshape(8 * size, size)
        field[x : x + 8] = jnp.dot(
            values,
            depth_ref[...],
            precision=lax.Precision.HIGHEST,
            preferred_element_type=jnp.float32,
        ).reshape(8, size, 128)
    zero = jnp.zeros((8, 128), jnp.float32)
    rows[PLANES - 1] = jnp.zeros_like(rows[0])

    def chunk(c, carry):
        here = pl.ds(pl.multiple_of(c * 8, 8), 8)
        there = pl.ds(pl.multiple_of(c * 8 + size, 8), 8)

        def load(x):
            tap = (x + size // 2) % WINDOW
            return field[tap, here, :] if tap < size else zero

        def store(plane, real, imag):
            rows[plane, here, :] = real
            rows[plane, there, :] = imag

        rows_forward(load, store, zero)
        return carry

    lax.fori_loop(0, size // 8, chunk, 0)
    lane = lax.broadcasted_iota(jnp.int32, (1, 128), 1)
    real_lane = lane <= 64
    first_half = lane < 64
    alone = (lane == 0) | (lane == 64)
    copies = []
    for p in range(0, PLANES, 2):
        both = along_columns(column_ref[...], jnp.concatenate([rows[p], rows[p + 1]], 1))
        for k in range(2):
            spectrum = both[:, 128 * k : 128 * (k + 1)]
            other = pltpu.roll(spectrum, 64, 1)
            factors[p + k, :128, :] = jnp.where(real_lane, spectrum, other)
            factors[p + k, 128:, :] = jnp.where(
                alone, 0.0, jnp.where(first_half, -other, spectrum)
            )
        if p + 2 in (PLANES // 2 + 1, PLANES):
            part = pl.ds(0, p + 2) if not copies else pl.ds(PLANES // 2 + 1, PLANES // 2 - 1)
            copies.append(
                pltpu.make_async_copy(
                    factors.at[part], out_ref.at[part], done.at[len(copies)]
                )
            )
            copies[-1].start()
    for copy in copies:
        copy.wait()


def convolve_kernel(
    adjoint,
    own_ref,
    top_ref,
    bottom_ref,
    left_ref,
    right_ref,
    transfer_ref,
    other_ref,
    depth_ref,
    column_ref,
    column_back_ref,
    depth_back_ref,
    out_ref,
    field,
    rows,
    back,
    factors,
    arrived,
):
    fetch = pltpu.make_async_copy(transfer_ref, factors, arrived)
    fetch.start()
    depth_matrix = depth_ref[...]

    def depth_piece(ref, x_from, y_from, step):
        count, width, lanes = ref.shape
        for x in range(0, count, step):
            values = ref[x : x + step].reshape(step * width, lanes)
            field[x_from + x : x_from + x + step, y_from : y_from + width, :] = along_depth(
                values, depth_matrix
            ).reshape(step, width, lanes)

    depth_piece(own_ref, 16, 16, 16)
    depth_piece(top_ref, 0, 16, 16)
    depth_piece(bottom_ref, 48, 16, 16)
    depth_piece(left_ref, 0, 0, 32)
    depth_piece(right_ref, 0, 48, 32)

    zero = jnp.zeros((8, 128), jnp.float32)
    rows[PLANES - 1] = jnp.zeros_like(rows[0])

    def chunk(c, carry):
        here = pl.ds(pl.multiple_of(c * 8, 8), 8)
        there = pl.ds(pl.multiple_of(c * 8 + WINDOW, 8), 8)

        def load(x):
            return field[x, here, :]

        def store(plane, real, imag):
            rows[plane, here, :] = real
            rows[plane, there, :] = imag

        rows_forward(load, store, zero)
        return carry

    lax.fori_loop(0, WINDOW // 8, chunk, 0)

    for p in range(0, PLANES, 2):
        spectrum = along_columns(
            column_ref[...], jnp.concatenate([rows[p], rows[p + 1]], 1)
        )
        rows[p] = spectrum[:, :128]
        rows[p + 1] = spectrum[:, 128:]

    fetch.wait()
    for p in range(0, PLANES, 2):
        weighted = []
        for k in range(2):
            own = rows[p + k]
            partner = pltpu.roll(own, 64, 1)
            a, b = own[:64], own[64:]
            c, d = partner[:64], partner[64:]
            fr, fi = factors[p + k, 0:64, :], factors[p + k, 64:128, :]
            gr, gi = factors[p + k, 128:192, :], factors[p + k, 192:256, :]
            if adjoint:
                real = (a * fr + b * fi) - (c * gr + d * gi)
                imag = (b * fr - a * fi) - (d * gr - c * gi)
            else:
                real = (a * fr - b * fi) + (c * gr - d * gi)
                imag = (b * fr + a * fi) + (d * gr + c * gi)
            weighted.append(jnp.concatenate([real, imag], 0))
        result = along_columns(column_back_ref[...], jnp.concatenate(weighted, 1))
        back[p] = result[:, :128]
        back[p + 1] = result[:, 128:]

    def chunk_back(c, carry):
        here = pl.ds(pl.multiple_of(c * 8, 8), 8)
        there = pl.ds(pl.multiple_of(c * 8 + 32, 8), 8)

        def load(plane):
            return back[plane, here, :], back[plane, there, :]

        def store(x, value):
            field[x, here, :] = value

        rows_inverse(load, store)
        return carry

    lax.fori_loop(0, 4, chunk_back, 0)

    matrix = depth_back_ref[...]
    for x in range(0, 32, 16):
        values = field[16 + x : 32 + x, 0:32, :].reshape(512, 128)
        result = along_depth(values, matrix).reshape(16, 32, 128)
        if adjoint:
            out_ref[x : x + 16] = other_ref[x : x + 16] * result
        else:
            out_ref[x : x + 16] = other_ref[x : x + 16] / result


def vmem(count):
    return [pl.BlockSpec(memory_space=pltpu.VMEM)] * count


def transfer_function(psf, depth):
    size = psf.shape[0]
    offsets = np.arange(size) - size // 2
    return pl.pallas_call(
        transfer_kernel,
        out_shape=jax.ShapeDtypeStruct((PLANES, 256, depth), jnp.float32),
        out_specs=pl.BlockSpec(memory_space=pltpu.HBM),
        scratch_shapes=[
            pltpu.VMEM((size, size, depth), jnp.float32),
            pltpu.VMEM((PLANES, 2 * size, depth), jnp.float32),
            pltpu.VMEM((PLANES, 256, depth), jnp.float32),
            pltpu.SemaphoreType.DMA((2,)),
        ],
        compiler_params=pltpu.CompilerParams(vmem_limit_bytes=16 * 2**20),
        name="transfer",
    )(
        psf,
        jnp.asarray(depth_forward(offsets, depth), jnp.float32),
        left_operand(column_forward(offsets)),
    )


def convolve(pieces, transfer, other, adjoint):
    depth = other.shape[2]
    positions = np.arange(WINDOW)
    scale = 1.0 / (WINDOW * WINDOW * depth)
    return pl.pallas_call(
        functools.partial(convolve_kernel, adjoint),
        out_shape=jax.ShapeDtypeStruct(other.shape, jnp.float32),
        in_specs=vmem(5) + [pl.BlockSpec(memory_space=pltpu.HBM)] + vmem(5),
        out_specs=pl.BlockSpec(memory_space=pltpu.VMEM),
        scratch_shapes=[
            pltpu.VMEM((WINDOW, WINDOW, depth), jnp.float32),
            pltpu.VMEM((PLANES, 2 * WINDOW, depth), jnp.float32),
            pltpu.VMEM((PLANES, WINDOW, depth), jnp.float32),
            pltpu.VMEM((PLANES, 256, depth), jnp.float32),
            pltpu.SemaphoreType.DMA,
        ],
        compiler_params=pltpu.CompilerParams(vmem_limit_bytes=20 * 2**20),
        name="correlate" if adjoint else "convolve",
    )(
        *pieces,
        transfer,
        other,
        right_operand(depth_forward(np.arange(depth), depth)),
        left_operand(column_forward(positions)),
        left_operand(column_inverse(positions[16:48])),
        right_operand(depth_inverse(depth) * scale),
    )


def halos(block, beside=None):
    def ring(axis, step):
        count = lax.axis_size(axis)
        return [(i, (i + step) % count) for i in range(count)]

    top = lax.ppermute(block[16:], "px", ring("px", 1))
    bottom = lax.ppermute(block[:16], "px", ring("px", -1))
    sent = block
    if beside is not None:
        sent, beside = lax.optimization_barrier((block, beside))
    ends = jnp.concatenate([top[:, 16:], sent[:, 16:], bottom[:, 16:]], 0)
    starts = jnp.concatenate([top[:, :16], sent[:, :16], bottom[:, :16]], 0)
    left = lax.ppermute(ends, "py", ring("py", 1))
    right = lax.ppermute(starts, "py", ring("py", -1))
    return (block, top, bottom, left, right), beside


def variation(pieces):
    volume, top, bottom, left, right = pieces
    row_count, col_count, _ = volume.shape
    row_whole = row_count * lax.axis_size("px")
    col_whole = col_count * lax.axis_size("py")
    padded = jnp.concatenate(
        [
            left[15:49, 15:],
            jnp.concatenate([top[15:], volume, bottom[:1]], 0),
            right[15:49, :1],
        ],
        1,
    )
    region = padded[:-1, :-1]
    slope_rows = padded[1:, :-1] - region
    slope_cols = padded[:-1, 1:] - region
    row_global = lax.axis_index("px") * row_count - 1 + jnp.arange(row_count + 1)
    col_global = lax.axis_index("py") * col_count - 1 + jnp.arange(col_count + 1)
    row_valid = ((row_global >= 0) & (row_global <= row_whole - 2))[:, None, None]
    col_valid = ((col_global >= 0) & (col_global <= col_whole - 2))[None, :, None]
    slope_rows = jnp.where(row_valid, slope_rows, 0.0)
    slope_cols = jnp.where(col_valid, slope_cols, 0.0)
    slope_depth = jnp.concatenate(
        [region[:, :, 1:] - region[:, :, :-1], jnp.zeros_like(region[:, :, :1])], 2
    )
    factor = lax.rsqrt(
        slope_rows * slope_rows
        + slope_cols * slope_cols
        + slope_depth * slope_depth
        + smoothing * smoothing
    )
    flux_rows, flux_cols = slope_rows * factor, slope_cols * factor
    flux_depth = (slope_depth * factor)[1:, 1:]
    flux_depth = flux_depth - jnp.concatenate(
        [jnp.zeros_like(flux_depth[:, :, :1]), flux_depth[:, :, :-1]], 2
    )
    return (
        flux_rows[1:, 1:]
        - flux_rows[:-1, 1:]
        + (flux_cols[1:, 1:] - flux_cols[1:, :-1])
        + flux_depth
    )


def shards(estimate, observed, psf):
    transfer = transfer_function(psf, estimate.shape[2])
    pieces, transfer = halos(estimate, transfer)
    quotient = convolve(pieces, transfer, observed, False)
    scaled = estimate / (1.0 - penalty_weight * variation(pieces))
    return convolve(halos(quotient)[0], transfer, scaled, True)


def solution(mesh):
    placed = (P("px", "py", None), P("px", "py", None), P())
    return jax.shard_map(
        shards, mesh=mesh, in_specs=placed, out_specs=P("px", "py", None), check_vma=False
    )
```

```python
import functools
import math

import jax
import jax.numpy as jnp
import ml_dtypes
import numpy as np
from jax import lax
from jax.experimental import pallas as pl
from jax.experimental.pallas import tpu as pltpu
from jax.sharding import PartitionSpec as P

penalty_weight = 0.1
smoothing = 0.1

WINDOW = 64
PLANES = 34
ROOT = math.sqrt(0.5)


def two_part(matrix):
    high = matrix.astype(ml_dtypes.bfloat16)
    low = (matrix - high.astype(np.float64)).astype(ml_dtypes.bfloat16)
    return high, low


def right_operand(matrix):
    high, low = two_part(matrix)
    return np.block([[high, low], [high, np.zeros_like(high)]])


def left_operand(matrix):
    high, low = two_part(matrix)
    return np.block([[high, high], [low, np.zeros_like(high)]])


def depth_forward(positions, depth):
    half = depth // 2
    turns = 2.0 * np.pi / depth
    real = np.cos(turns * np.outer(positions, np.arange(half + 1)))
    imag = -np.sin(turns * np.outer(positions, np.arange(1, half)))
    return np.concatenate([real, imag], 1)


def depth_inverse(depth):
    half = depth // 2
    turns = 2.0 * np.pi / depth
    positions = np.arange(depth)
    weight = np.full(half + 1, 2.0)
    weight[0] = weight[half] = 1.0
    real = weight[:, None] * np.cos(turns * np.outer(np.arange(half + 1), positions))
    imag = -2.0 * np.sin(turns * np.outer(np.arange(1, half), positions))
    return np.concatenate([real, imag], 0)


def column_forward(positions):
    angles = 2.0 * np.pi / WINDOW * np.outer(np.arange(WINDOW), positions)
    cosine, sine = np.cos(angles), np.sin(angles)
    return np.block([[cosine, sine], [-sine, cosine]])


def column_inverse(positions):
    angles = 2.0 * np.pi / WINDOW * np.outer(positions, np.arange(WINDOW))
    cosine, sine = np.cos(angles), np.sin(angles)
    return np.block([[cosine, -sine], [sine, cosine]])


def add(a, b):
    return (a[0] + b[0], a[1] + b[1])


def sub(a, b):
    return (a[0] - b[0], a[1] - b[1])


def turn(a, eighths):
    real, imag = a
    eighths %= 8
    if eighths == 0:
        return a
    if eighths == 2:
        return (-imag, real)
    if eighths == 4:
        return (-real, -imag)
    if eighths == 6:
        return (imag, -real)
    total, gap = (real + imag) * ROOT, (real - imag) * ROOT
    if eighths == 1:
        return (gap, total)
    if eighths == 3:
        return (-total, gap)
    if eighths == 5:
        return (-gap, -total)
    return (total, -gap)


def twiddle(a, power, sign):
    angle = sign * 2.0 * math.pi * power / WINDOW
    cosine, sine = math.cos(angle), math.sin(angle)
    if power == 0:
        return a
    real, imag = a
    return (real * cosine - imag * sine, real * sine + imag * cosine)


def complex_eight(values, sign):
    if len(values) == 1:
        return values
    count = len(values)
    even = complex_eight(values[0::2], sign)
    odd = complex_eight(values[1::2], sign)
    odd = [turn(value, sign * k * (8 // count)) for k, value in enumerate(odd)]
    return [add(e, o) for e, o in zip(even, odd)] + [sub(e, o) for e, o in zip(even, odd)]


def real_eight(a):
    s04, d04, s26, d26 = a[0] + a[4], a[0] - a[4], a[2] + a[6], a[2] - a[6]
    s15, d15, s37, d37 = a[1] + a[5], a[1] - a[5], a[3] + a[7], a[3] - a[7]
    even, odd = s04 + s26, s15 + s37
    gap, total = (d15 - d37) * ROOT, (d15 + d37) * ROOT
    return (
        even + odd,
        (d04 + gap, -d26 - total),
        (s04 - s26, s37 - s15),
        (d04 - gap, d26 - total),
        even - odd,
    )


def rows_forward(load, store, zero):
    first = [real_eight([load(8 * x1 + x0) for x1 in range(8)]) for x0 in range(8)]
    ends = real_eight([f[0] for f in first])
    store(0, ends[0], zero)
    for k0 in (1, 2, 3):
        store(k0, *ends[k0])
    store(4, ends[4], zero)
    plane = 5
    for k1 in (1, 2, 3):
        out = complex_eight([twiddle(first[x0][k1], k1 * x0, -1) for x0 in range(8)], -1)
        for value in out:
            store(plane, *value)
            plane += 1
    middle = []
    for x0 in range(8):
        angle = 2.0 * math.pi * 4 * x0 / WINDOW
        middle.append((first[x0][4] * math.cos(angle), first[x0][4] * -math.sin(angle)))
    middle = complex_eight(middle, -1)
    for k0 in range(4):
        store(plane, *middle[k0])
        plane += 1


def rows_inverse(load, store):
    ends = [load(p) for p in range(5)]
    x0r, x4r = ends[0][0], ends[4][0]
    spectrum = [(x0r, jnp.zeros_like(x0r))] + [ends[k] for k in (1, 2, 3)]
    parts = [[None] * 8 for _ in range(5)]
    (r1, i1), (r2, i2), (r3, i3) = [(2.0 * e[0], 2.0 * e[1]) for e in ends[1:4]]
    del spectrum
    base, flip = x0r + x4r, x0r - x4r
    g13, t13 = r1 - r3, r1 + r3
    h13, u13 = i1 - i3, i1 + i3
    parts[0][0] = base + t13 + r2
    parts[0][4] = base - t13 + r2
    parts[0][2] = base - r2 - h13
    parts[0][6] = base - r2 + h13
    odd_a, odd_b = g13 * ROOT, u13 * ROOT
    parts[0][1] = flip + odd_a - odd_b - i2
    parts[0][5] = flip - odd_a + odd_b - i2
    parts[0][3] = flip - odd_a - odd_b + i2
    parts[0][7] = flip + odd_a + odd_b + i2
    plane = 5
    for k1 in (1, 2, 3):
        values = complex_eight([load(plane + k0) for k0 in range(8)], 1)
        plane += 8
        parts[k1] = [twiddle(values[x0], k1 * x0, 1) for x0 in range(8)]
    half = [load(plane + k0) for k0 in range(4)]
    middle = complex_eight(half + [(half[3 - k][0], -half[3 - k][1]) for k in range(4)], 1)
    for x0 in range(8):
        angle = 2.0 * math.pi * 4 * x0 / WINDOW
        parts[4][x0] = middle[x0][0] * math.cos(angle) - middle[x0][1] * math.sin(angle)
    for x0 in range(8):
        v0, v4 = parts[0][x0], parts[4][x0]
        (a, b), (c, d), (e, f) = parts[1][x0], parts[2][x0], parts[3][x0]
        plus, minus = v0 + v4, v0 - v4
        store(16 + x0, plus + 2.0 * (f - b - c))
        store(24 + x0, minus + 2.0 * (d + ROOT * ((e - f) - (a + b))))
        store(32 + x0, plus + 2.0 * (c - a - e))
        store(40 + x0, minus + 2.0 * (ROOT * ((b - a) + (e + f)) - d))


def parts_of(value):
    high = value.astype(jnp.bfloat16)
    low = (value - high.astype(jnp.float32)).astype(jnp.bfloat16)
    return high, low


def along_depth(rows, matrix):
    high, low = parts_of(rows)
    out = jnp.dot(
        jnp.concatenate([high, low], 1), matrix, preferred_element_type=jnp.float32
    )
    return out[:, :128] + out[:, 128:]


def along_columns(matrix, value):
    high, low = parts_of(value)
    out = jnp.dot(
        matrix, jnp.concatenate([high, low], 0), preferred_element_type=jnp.float32
    )
    half = out.shape[0] // 2
    return out[:half] + out[half:]


def transfer_kernel(psf_ref, depth_ref, column_ref, factors, field, rows):
    size = psf_ref.shape[0]
    for x in range(0, size, 8):
        values = psf_ref[x : x + 8].reshape(8 * size, size)
        field[x : x + 8] = jnp.dot(
            values,
            depth_ref[...],
            precision=lax.Precision.HIGHEST,
            preferred_element_type=jnp.float32,
        ).reshape(8, size, 128)
    zero = jnp.zeros((8, 128), jnp.float32)
    rows[PLANES - 1] = jnp.zeros_like(rows[0])

    def chunk(c, carry):
        here = pl.ds(pl.multiple_of(c * 8, 8), 8)
        there = pl.ds(pl.multiple_of(c * 8 + size, 8), 8)

        def load(x):
            tap = (x + size // 2) % WINDOW
            return field[tap, here, :] if tap < size else zero

        def store(plane, real, imag):
            rows[plane, here, :] = real
            rows[plane, there, :] = imag

        rows_forward(load, store, zero)
        return carry

    lax.fori_loop(0, size // 8, chunk, 0)
    lane = lax.broadcasted_iota(jnp.int32, (1, 128), 1)
    real_lane = lane <= 64
    first_half = lane < 64
    alone = (lane == 0) | (lane == 64)
    for p in range(0, PLANES, 2):
        both = along_columns(column_ref[...], jnp.concatenate([rows[p], rows[p + 1]], 1))
        for k in range(2):
            spectrum = both[:, 128 * k : 128 * (k + 1)]
            other = pltpu.roll(spectrum, 64, 1)
            factors[p + k, :128, :] = jnp.where(real_lane, spectrum, other)
            factors[p + k, 128:, :] = jnp.where(
                alone, 0.0, jnp.where(first_half, -other, spectrum)
            )


def depth_piece(ref, matrix, field, x_from, y_from):
    count, width, lanes = ref.shape
    step = 512 // width
    for x in range(0, count, step):
        values = ref[x : x + step].reshape(step * width, lanes)
        field[x_from + x : x_from + x + step, y_from : y_from + width, :] = along_depth(
            values, matrix
        ).reshape(step, width, lanes)


def row_transforms(field, rows, width):
    zero = jnp.zeros((8, 128), jnp.float32)
    rows[PLANES - 1] = jnp.zeros_like(rows[0])

    def chunk(c, carry):
        here = pl.ds(pl.multiple_of(c * 8, 8), 8)
        there = pl.ds(pl.multiple_of(c * 8 + width, 8), 8)

        def load(x):
            return field[x, here, :]

        def store(plane, real, imag):
            rows[plane, here, :] = real
            rows[plane, there, :] = imag

        rows_forward(load, store, zero)
        return carry

    lax.fori_loop(0, width // 8, chunk, 0)


def edges_kernel(own_ref, above_ref, below_ref, ends_ref, starts_ref):
    for ref, at in ((above_ref, 0), (own_ref, 16), (below_ref, 48)):
        count = ref.shape[0]
        ends_ref[at : at + count] = ref[:, 16:, :]
        starts_ref[at : at + count] = ref[:, :16, :]


def inner_kernel(own_ref, above_ref, below_ref, depth_ref, rows_ref, field):
    matrix = depth_ref[...]
    depth_piece(own_ref, matrix, field, 16, 0)
    depth_piece(above_ref, matrix, field, 0, 0)
    depth_piece(below_ref, matrix, field, 48, 0)
    row_transforms(field, rows_ref, 32)


def convolve_kernel(
    adjoint,
    inner_ref,
    left_ref,
    right_ref,
    transfer_ref,
    other_ref,
    depth_ref,
    column_ref,
    column_back_ref,
    depth_back_ref,
    out_ref,
    field,
    rows,
    spectra,
    back,
):
    depth_matrix = depth_ref[...]
    depth_piece(left_ref, depth_matrix, field, 0, 0)
    depth_piece(right_ref, depth_matrix, field, 0, 16)
    row_transforms(field, rows, 32)

    for p in range(0, PLANES, 2):
        spectrum = along_columns(
            column_ref[...],
            jnp.concatenate(
                [
                    jnp.concatenate([inner_ref[p], rows[p]], 0),
                    jnp.concatenate([inner_ref[p + 1], rows[p + 1]], 0),
                ],
                1,
            ),
        )
        spectra[p] = spectrum[:, :128]
        spectra[p + 1] = spectrum[:, 128:]

    for p in range(0, PLANES, 2):
        weighted = []
        for k in range(2):
            own = spectra[p + k]
            partner = pltpu.roll(own, 64, 1)
            a, b = own[:64], own[64:]
            c, d = partner[:64], partner[64:]
            fr, fi = transfer_ref[p + k, 0:64, :], transfer_ref[p + k, 64:128, :]
            gr, gi = transfer_ref[p + k, 128:192, :], transfer_ref[p + k, 192:256, :]
            if adjoint:
                real = (a * fr + b * fi) - (c * gr + d * gi)
                imag = (b * fr - a * fi) - (d * gr - c * gi)
            else:
                real = (a * fr - b * fi) + (c * gr - d * gi)
                imag = (b * fr + a * fi) + (d * gr + c * gi)
            weighted.append(jnp.concatenate([real, imag], 0))
        result = along_columns(column_back_ref[...], jnp.concatenate(weighted, 1))
        back[p] = result[:, :128]
        back[p + 1] = result[:, 128:]

    def chunk_back(c, carry):
        here = pl.ds(pl.multiple_of(c * 8, 8), 8)
        there = pl.ds(pl.multiple_of(c * 8 + 32, 8), 8)

        def load(plane):
            return back[plane, here, :], back[plane, there, :]

        def store(x, value):
            field[x, here, :] = value

        rows_inverse(load, store)
        return carry

    lax.fori_loop(0, 4, chunk_back, 0)

    matrix = depth_back_ref[...]
    for x in range(0, 32, 16):
        values = field[16 + x : 32 + x].reshape(512, 128)
        result = along_depth(values, matrix).reshape(16, 32, 128)
        if adjoint:
            out_ref[x : x + 16] = other_ref[x : x + 16] * result
        else:
            out_ref[x : x + 16] = other_ref[x : x + 16] / result


def vmem(count):
    return [pl.BlockSpec(memory_space=pltpu.VMEM)] * count


def transfer_function(psf, depth):
    size = psf.shape[0]
    offsets = np.arange(size) - size // 2
    return pl.pallas_call(
        transfer_kernel,
        out_shape=jax.ShapeDtypeStruct((PLANES, 256, depth), jnp.float32),
        out_specs=vmem(1)[0],
        scratch_shapes=[
            pltpu.VMEM((size, size, depth), jnp.float32),
            pltpu.VMEM((PLANES, 2 * size, depth), jnp.float32),
        ],
        compiler_params=pltpu.CompilerParams(vmem_limit_bytes=16 * 2**20),
        name="transfer",
    )(
        psf,
        jnp.asarray(depth_forward(offsets, depth), jnp.float32),
        left_operand(column_forward(offsets)),
    )


def edges(own, above, below):
    shape = jax.ShapeDtypeStruct((WINDOW, 16, own.shape[2]), jnp.float32)
    return pl.pallas_call(
        edges_kernel,
        out_shape=(shape, shape),
        in_specs=vmem(3),
        out_specs=tuple(vmem(2)),
        compiler_params=pltpu.CompilerParams(vmem_limit_bytes=2 * 2**20),
        name="edges",
    )(own, above, below)


def convolve(pieces, transfer, other, adjoint):
    own, above, below, left, right = pieces
    depth = other.shape[2]
    positions = np.arange(WINDOW)
    scale = 1.0 / (WINDOW * WINDOW * depth)
    depth_matrix = right_operand(depth_forward(np.arange(depth), depth))
    half_rows = (PLANES, WINDOW, depth)
    inner = pl.pallas_call(
        inner_kernel,
        out_shape=jax.ShapeDtypeStruct(half_rows, jnp.float32),
        in_specs=vmem(4),
        out_specs=vmem(1)[0],
        scratch_shapes=[pltpu.VMEM((WINDOW, 32, depth), jnp.float32)],
        compiler_params=pltpu.CompilerParams(vmem_limit_bytes=16 * 2**20),
        name="inner",
    )(own, above, below, depth_matrix)
    forward = np.concatenate(
        [
            column_forward(positions[16:48]),
            column_forward(np.concatenate([positions[:16], positions[48:]])),
        ],
        1,
    )
    return pl.pallas_call(
        functools.partial(convolve_kernel, adjoint),
        out_shape=jax.ShapeDtypeStruct(other.shape, jnp.float32),
        in_specs=vmem(9),
        out_specs=vmem(1)[0],
        scratch_shapes=[
            pltpu.VMEM((WINDOW, 32, depth), jnp.float32),
            pltpu.VMEM(half_rows, jnp.float32),
            pltpu.VMEM((PLANES, 2 * WINDOW, depth), jnp.float32),
            pltpu.VMEM(half_rows, jnp.float32),
        ],
        compiler_params=pltpu.CompilerParams(vmem_limit_bytes=20 * 2**20),
        name="correlate" if adjoint else "convolve",
    )(
        inner,
        left,
        right,
        transfer,
        other,
        depth_matrix,
        left_operand(forward),
        left_operand(column_inverse(positions[16:48])),
        right_operand(depth_inverse(depth) * scale),
    )


def halos(block):
    def ring(axis, step):
        count = lax.axis_size(axis)
        return [(i, (i + step) % count) for i in range(count)]

    above = lax.ppermute(block[16:], "px", ring("px", 1))
    below = lax.ppermute(block[:16], "px", ring("px", -1))
    ends, starts = edges(block, above, below)
    left = lax.ppermute(ends, "py", ring("py", 1))
    right = lax.ppermute(starts, "py", ring("py", -1))
    return block, above, below, left, right


def variation(pieces):
    volume, above, below, left, right = pieces
    row_count, col_count, _ = volume.shape
    row_whole = row_count * lax.axis_size("px")
    col_whole = col_count * lax.axis_size("py")
    padded = jnp.concatenate(
        [
            left[15:49, 15:],
            jnp.concatenate([above[15:], volume, below[:1]], 0),
            right[15:49, :1],
        ],
        1,
    )
    region = padded[:-1, :-1]
    slope_rows = padded[1:, :-1] - region
    slope_cols = padded[:-1, 1:] - region
    row_global = lax.axis_index("px") * row_count - 1 + jnp.arange(row_count + 1)
    col_global = lax.axis_index("py") * col_count - 1 + jnp.arange(col_count + 1)
    row_valid = ((row_global >= 0) & (row_global <= row_whole - 2))[:, None, None]
    col_valid = ((col_global >= 0) & (col_global <= col_whole - 2))[None, :, None]
    slope_rows = jnp.where(row_valid, slope_rows, 0.0)
    slope_cols = jnp.where(col_valid, slope_cols, 0.0)
    slope_depth = jnp.concatenate(
        [region[:, :, 1:] - region[:, :, :-1], jnp.zeros_like(region[:, :, :1])], 2
    )
    factor = lax.rsqrt(
        slope_rows * slope_rows
        + slope_cols * slope_cols
        + slope_depth * slope_depth
        + smoothing * smoothing
    )
    flux_rows, flux_cols = slope_rows * factor, slope_cols * factor
    flux_depth = (slope_depth * factor)[1:, 1:]
    flux_depth = flux_depth - jnp.concatenate(
        [jnp.zeros_like(flux_depth[:, :, :1]), flux_depth[:, :, :-1]], 2
    )
    return (
        flux_rows[1:, 1:]
        - flux_rows[:-1, 1:]
        + (flux_cols[1:, 1:] - flux_cols[1:, :-1])
        + flux_depth
    )


def shards(estimate, observed, psf):
    transfer = transfer_function(psf, estimate.shape[2])
    pieces = halos(estimate)
    quotient = convolve(pieces, transfer, observed, False)
    scaled = estimate / (1.0 - penalty_weight * variation(pieces))
    return convolve(halos(quotient), transfer, scaled, True)


def solution(mesh):
    placed = (P("px", "py", None), P("px", "py", None), P())
    return jax.shard_map(
        shards, mesh=mesh, in_specs=placed, out_specs=P("px", "py", None), check_vma=False
    )
```

```python
import functools
import math

import jax
import jax.numpy as jnp
import ml_dtypes
import numpy as np
from jax import lax
from jax.experimental import pallas as pl
from jax.experimental.pallas import tpu as pltpu
from jax.sharding import PartitionSpec as P

penalty_weight = 0.1
smoothing = 0.1

WINDOW = 64
PLANES = 34
ROOT = math.sqrt(0.5)


def two_part(matrix):
    high = matrix.astype(ml_dtypes.bfloat16)
    low = (matrix - high.astype(np.float64)).astype(ml_dtypes.bfloat16)
    return high, low


def right_operand(matrix):
    high, low = two_part(matrix)
    return np.block([[high, low], [high, np.zeros_like(high)]])


def left_operand(matrix):
    high, low = two_part(matrix)
    return np.block([[high, high], [low, np.zeros_like(high)]])


def depth_forward(positions, depth):
    half = depth // 2
    turns = 2.0 * np.pi / depth
    real = np.cos(turns * np.outer(positions, np.arange(half + 1)))
    imag = -np.sin(turns * np.outer(positions, np.arange(1, half)))
    return np.concatenate([real, imag], 1)


def depth_inverse(depth):
    half = depth // 2
    turns = 2.0 * np.pi / depth
    positions = np.arange(depth)
    weight = np.full(half + 1, 2.0)
    weight[0] = weight[half] = 1.0
    real = weight[:, None] * np.cos(turns * np.outer(np.arange(half + 1), positions))
    imag = -2.0 * np.sin(turns * np.outer(np.arange(1, half), positions))
    return np.concatenate([real, imag], 0)


def column_forward(positions):
    angles = 2.0 * np.pi / WINDOW * np.outer(np.arange(WINDOW), positions)
    cosine, sine = np.cos(angles), np.sin(angles)
    return np.block([[cosine, sine], [-sine, cosine]])


def column_inverse(positions):
    angles = 2.0 * np.pi / WINDOW * np.outer(positions, np.arange(WINDOW))
    cosine, sine = np.cos(angles), np.sin(angles)
    return np.block([[cosine, -sine], [sine, cosine]])


def add(a, b):
    return (a[0] + b[0], a[1] + b[1])


def sub(a, b):
    return (a[0] - b[0], a[1] - b[1])


def turn(a, eighths):
    real, imag = a
    eighths %= 8
    if eighths == 0:
        return a
    if eighths == 2:
        return (-imag, real)
    if eighths == 4:
        return (-real, -imag)
    if eighths == 6:
        return (imag, -real)
    total, gap = (real + imag) * ROOT, (real - imag) * ROOT
    if eighths == 1:
        return (gap, total)
    if eighths == 3:
        return (-total, gap)
    if eighths == 5:
        return (-gap, -total)
    return (total, -gap)


def twiddle(a, power, sign):
    angle = sign * 2.0 * math.pi * power / WINDOW
    cosine, sine = math.cos(angle), math.sin(angle)
    if power == 0:
        return a
    real, imag = a
    return (real * cosine - imag * sine, real * sine + imag * cosine)


def complex_eight(values, sign):
    if len(values) == 1:
        return values
    count = len(values)
    even = complex_eight(values[0::2], sign)
    odd = complex_eight(values[1::2], sign)
    odd = [turn(value, sign * k * (8 // count)) for k, value in enumerate(odd)]
    return [add(e, o) for e, o in zip(even, odd)] + [sub(e, o) for e, o in zip(even, odd)]


def real_eight(a):
    s04, d04, s26, d26 = a[0] + a[4], a[0] - a[4], a[2] + a[6], a[2] - a[6]
    s15, d15, s37, d37 = a[1] + a[5], a[1] - a[5], a[3] + a[7], a[3] - a[7]
    even, odd = s04 + s26, s15 + s37
    gap, total = (d15 - d37) * ROOT, (d15 + d37) * ROOT
    return (
        even + odd,
        (d04 + gap, -d26 - total),
        (s04 - s26, s37 - s15),
        (d04 - gap, d26 - total),
        even - odd,
    )


def rows_forward(load, store, zero):
    first = [real_eight([load(8 * x1 + x0) for x1 in range(8)]) for x0 in range(8)]
    ends = real_eight([f[0] for f in first])
    store(0, ends[0], zero)
    for k0 in (1, 2, 3):
        store(k0, *ends[k0])
    store(4, ends[4], zero)
    plane = 5
    for k1 in (1, 2, 3):
        out = complex_eight([twiddle(first[x0][k1], k1 * x0, -1) for x0 in range(8)], -1)
        for value in out:
            store(plane, *value)
            plane += 1
    middle = []
    for x0 in range(8):
        angle = 2.0 * math.pi * 4 * x0 / WINDOW
        middle.append((first[x0][4] * math.cos(angle), first[x0][4] * -math.sin(angle)))
    middle = complex_eight(middle, -1)
    for k0 in range(4):
        store(plane, *middle[k0])
        plane += 1


def rows_inverse(load, store):
    ends = [load(p) for p in range(5)]
    x0r, x4r = ends[0][0], ends[4][0]
    spectrum = [(x0r, jnp.zeros_like(x0r))] + [ends[k] for k in (1, 2, 3)]
    parts = [[None] * 8 for _ in range(5)]
    (r1, i1), (r2, i2), (r3, i3) = [(2.0 * e[0], 2.0 * e[1]) for e in ends[1:4]]
    del spectrum
    base, flip = x0r + x4r, x0r - x4r
    g13, t13 = r1 - r3, r1 + r3
    h13, u13 = i1 - i3, i1 + i3
    parts[0][0] = base + t13 + r2
    parts[0][4] = base - t13 + r2
    parts[0][2] = base - r2 - h13
    parts[0][6] = base - r2 + h13
    odd_a, odd_b = g13 * ROOT, u13 * ROOT
    parts[0][1] = flip + odd_a - odd_b - i2
    parts[0][5] = flip - odd_a + odd_b - i2
    parts[0][3] = flip - odd_a - odd_b + i2
    parts[0][7] = flip + odd_a + odd_b + i2
    plane = 5
    for k1 in (1, 2, 3):
        values = complex_eight([load(plane + k0) for k0 in range(8)], 1)
        plane += 8
        parts[k1] = [twiddle(values[x0], k1 * x0, 1) for x0 in range(8)]
    half = [load(plane + k0) for k0 in range(4)]
    middle = complex_eight(half + [(half[3 - k][0], -half[3 - k][1]) for k in range(4)], 1)
    for x0 in range(8):
        angle = 2.0 * math.pi * 4 * x0 / WINDOW
        parts[4][x0] = middle[x0][0] * math.cos(angle) - middle[x0][1] * math.sin(angle)
    for x0 in range(8):
        v0, v4 = parts[0][x0], parts[4][x0]
        (a, b), (c, d), (e, f) = parts[1][x0], parts[2][x0], parts[3][x0]
        plus, minus = v0 + v4, v0 - v4
        store(16 + x0, plus + 2.0 * (f - b - c))
        store(24 + x0, minus + 2.0 * (d + ROOT * ((e - f) - (a + b))))
        store(32 + x0, plus + 2.0 * (c - a - e))
        store(40 + x0, minus + 2.0 * (ROOT * ((b - a) + (e + f)) - d))


def parts_of(value):
    high = value.astype(jnp.bfloat16)
    low = (value - high.astype(jnp.float32)).astype(jnp.bfloat16)
    return high, low


def along_depth(rows, matrix):
    high, low = parts_of(rows)
    out = jnp.dot(
        jnp.concatenate([high, low], 1), matrix, preferred_element_type=jnp.float32
    )
    return out[:, :128] + out[:, 128:]


def along_columns(matrix, value):
    high, low = parts_of(value)
    out = jnp.dot(
        matrix, jnp.concatenate([high, low], 0), preferred_element_type=jnp.float32
    )
    half = out.shape[0] // 2
    return out[:half] + out[half:]


def transfer_kernel(psf_ref, depth_ref, column_ref, factors, field, rows):
    size = psf_ref.shape[0]
    for x in range(0, size, 8):
        values = psf_ref[x : x + 8].reshape(8 * size, size)
        field[x : x + 8] = jnp.dot(
            values,
            depth_ref[...],
            precision=lax.Precision.HIGHEST,
            preferred_element_type=jnp.float32,
        ).reshape(8, size, 128)
    zero = jnp.zeros((8, 128), jnp.float32)
    rows[PLANES - 1] = jnp.zeros_like(rows[0])

    def chunk(c, carry):
        here = pl.ds(pl.multiple_of(c * 8, 8), 8)
        there = pl.ds(pl.multiple_of(c * 8 + size, 8), 8)

        def load(x):
            tap = (x + size // 2) % WINDOW
            return field[tap, here, :] if tap < size else zero

        def store(plane, real, imag):
            rows[plane, here, :] = real
            rows[plane, there, :] = imag

        rows_forward(load, store, zero)
        return carry

    lax.fori_loop(0, size // 8, chunk, 0)
    lane = lax.broadcasted_iota(jnp.int32, (1, 128), 1)
    real_lane = lane <= 64
    first_half = lane < 64
    alone = (lane == 0) | (lane == 64)
    for p in range(0, PLANES, 2):
        both = along_columns(column_ref[...], jnp.concatenate([rows[p], rows[p + 1]], 1))
        for k in range(2):
            spectrum = both[:, 128 * k : 128 * (k + 1)]
            other = pltpu.roll(spectrum, 64, 1)
            factors[p + k, :128, :] = jnp.where(real_lane, spectrum, other)
            factors[p + k, 128:, :] = jnp.where(
                alone, 0.0, jnp.where(first_half, -other, spectrum)
            )


def depth_piece(ref, matrix, field, x_from, y_from):
    count, width, lanes = ref.shape
    step = 512 // width
    for x in range(0, count, step):
        values = ref[x : x + step].reshape(step * width, lanes)
        field[x_from + x : x_from + x + step, y_from : y_from + width, :] = along_depth(
            values, matrix
        ).reshape(step, width, lanes)


def row_transforms(field, rows, width):
    zero = jnp.zeros((8, 128), jnp.float32)
    rows[PLANES - 1] = jnp.zeros_like(rows[0])

    def chunk(c, carry):
        here = pl.ds(pl.multiple_of(c * 8, 8), 8)
        there = pl.ds(pl.multiple_of(c * 8 + width, 8), 8)

        def load(x):
            return field[x, here, :]

        def store(plane, real, imag):
            rows[plane, here, :] = real
            rows[plane, there, :] = imag

        rows_forward(load, store, zero)
        return carry

    lax.fori_loop(0, width // 8, chunk, 0)


def edges_kernel(own_ref, above_ref, below_ref, ends_ref, starts_ref):
    for ref, at in ((above_ref, 0), (own_ref, 16), (below_ref, 48)):
        count = ref.shape[0]
        ends_ref[at : at + count] = ref[:, 16:, :]
        starts_ref[at : at + count] = ref[:, :16, :]


def split_kernel(block_ref, whole_ref, last_ref, first_ref, done):
    rows = (pl.ds(16, 16), last_ref), (pl.ds(0, 16), first_ref), (pl.ds(0, 32), whole_ref)
    copies = [
        pltpu.make_async_copy(block_ref.at[part], ref, done.at[i])
        for i, (part, ref) in enumerate(rows)
    ]
    for copy in copies:
        copy.start()
    for copy in copies:
        copy.wait()


def inner_kernel(own_ref, above_ref, below_ref, depth_ref, rows_ref, field):
    matrix = depth_ref[...]
    depth_piece(own_ref, matrix, field, 16, 0)
    depth_piece(above_ref, matrix, field, 0, 0)
    depth_piece(below_ref, matrix, field, 48, 0)
    row_transforms(field, rows_ref, 32)


def convolve_kernel(
    adjoint,
    inner_ref,
    left_ref,
    right_ref,
    transfer_ref,
    other_ref,
    depth_ref,
    column_ref,
    column_back_ref,
    depth_back_ref,
    out_ref,
    field,
    rows,
    spectra,
    back,
):
    depth_matrix = depth_ref[...]
    depth_piece(left_ref, depth_matrix, field, 0, 0)
    depth_piece(right_ref, depth_matrix, field, 0, 16)
    row_transforms(field, rows, 32)

    for p in range(0, PLANES, 2):
        spectrum = along_columns(
            column_ref[...],
            jnp.concatenate(
                [
                    jnp.concatenate([inner_ref[p], rows[p]], 0),
                    jnp.concatenate([inner_ref[p + 1], rows[p + 1]], 0),
                ],
                1,
            ),
        )
        spectra[p] = spectrum[:, :128]
        spectra[p + 1] = spectrum[:, 128:]

    for p in range(0, PLANES, 2):
        weighted = []
        for k in range(2):
            own = spectra[p + k]
            partner = pltpu.roll(own, 64, 1)
            a, b = own[:64], own[64:]
            c, d = partner[:64], partner[64:]
            fr, fi = transfer_ref[p + k, 0:64, :], transfer_ref[p + k, 64:128, :]
            gr, gi = transfer_ref[p + k, 128:192, :], transfer_ref[p + k, 192:256, :]
            if adjoint:
                real = (a * fr + b * fi) - (c * gr + d * gi)
                imag = (b * fr - a * fi) - (d * gr - c * gi)
            else:
                real = (a * fr - b * fi) + (c * gr - d * gi)
                imag = (b * fr + a * fi) + (d * gr + c * gi)
            weighted.append(jnp.concatenate([real, imag], 0))
        result = along_columns(column_back_ref[...], jnp.concatenate(weighted, 1))
        back[p] = result[:, :128]
        back[p + 1] = result[:, 128:]

    def chunk_back(c, carry):
        here = pl.ds(pl.multiple_of(c * 8, 8), 8)
        there = pl.ds(pl.multiple_of(c * 8 + 32, 8), 8)

        def load(plane):
            return back[plane, here, :], back[plane, there, :]

        def store(x, value):
            field[x, here, :] = value

        rows_inverse(load, store)
        return carry

    lax.fori_loop(0, 4, chunk_back, 0)

    matrix = depth_back_ref[...]
    for x in range(0, 32, 16):
        values = field[16 + x : 32 + x].reshape(512, 128)
        result = along_depth(values, matrix).reshape(16, 32, 128)
        if adjoint:
            out_ref[x : x + 16] = other_ref[x : x + 16] * result
        else:
            out_ref[x : x + 16] = other_ref[x : x + 16] / result


def vmem(count):
    return [pl.BlockSpec(memory_space=pltpu.VMEM)] * count


def transfer_function(psf, depth):
    size = psf.shape[0]
    offsets = np.arange(size) - size // 2
    return pl.pallas_call(
        transfer_kernel,
        out_shape=jax.ShapeDtypeStruct((PLANES, 256, depth), jnp.float32),
        out_specs=vmem(1)[0],
        scratch_shapes=[
            pltpu.VMEM((size, size, depth), jnp.float32),
            pltpu.VMEM((PLANES, 2 * size, depth), jnp.float32),
        ],
        compiler_params=pltpu.CompilerParams(vmem_limit_bytes=8 * 2**20),
        name="transfer",
    )(
        psf,
        jnp.asarray(depth_forward(offsets, depth), jnp.float32),
        left_operand(column_forward(offsets)),
    )


def edges(own, above, below):
    shape = jax.ShapeDtypeStruct((WINDOW, 16, own.shape[2]), jnp.float32)
    return pl.pallas_call(
        edges_kernel,
        out_shape=(shape, shape),
        in_specs=vmem(3),
        out_specs=tuple(vmem(2)),
        compiler_params=pltpu.CompilerParams(vmem_limit_bytes=2 * 2**20),
        name="edges",
    )(own, above, below)


def split(block):
    shape = jax.ShapeDtypeStruct((16,) + block.shape[1:], jnp.float32)
    return pl.pallas_call(
        split_kernel,
        out_shape=(jax.ShapeDtypeStruct(block.shape, jnp.float32), shape, shape),
        in_specs=[pl.BlockSpec(memory_space=pltpu.HBM)],
        out_specs=tuple(vmem(3)),
        scratch_shapes=[pltpu.SemaphoreType.DMA((3,))],
        compiler_params=pltpu.CompilerParams(vmem_limit_bytes=2**20),
        name="split",
    )(block)


def convolve(pieces, transfer, other, adjoint):
    own, above, below, left, right = pieces
    depth = other.shape[2]
    positions = np.arange(WINDOW)
    scale = 1.0 / (WINDOW * WINDOW * depth)
    depth_matrix = right_operand(depth_forward(np.arange(depth), depth))
    half_rows = (PLANES, WINDOW, depth)
    inner = pl.pallas_call(
        inner_kernel,
        out_shape=jax.ShapeDtypeStruct(half_rows, jnp.float32),
        in_specs=vmem(4),
        out_specs=vmem(1)[0],
        scratch_shapes=[pltpu.VMEM((WINDOW, 32, depth), jnp.float32)],
        compiler_params=pltpu.CompilerParams(vmem_limit_bytes=4 * 2**20),
        name="inner",
    )(own, above, below, depth_matrix)
    forward = np.concatenate(
        [
            column_forward(positions[16:48]),
            column_forward(np.concatenate([positions[:16], positions[48:]])),
        ],
        1,
    )
    return pl.pallas_call(
        functools.partial(convolve_kernel, adjoint),
        out_shape=jax.ShapeDtypeStruct(other.shape, jnp.float32),
        in_specs=vmem(9),
        out_specs=vmem(1)[0],
        scratch_shapes=[
            pltpu.VMEM((WINDOW, 32, depth), jnp.float32),
            pltpu.VMEM(half_rows, jnp.float32),
            pltpu.VMEM((PLANES, 2 * WINDOW, depth), jnp.float32),
            pltpu.VMEM(half_rows, jnp.float32),
        ],
        compiler_params=pltpu.CompilerParams(vmem_limit_bytes=20 * 2**20),
        name="correlate" if adjoint else "convolve",
    )(
        inner,
        left,
        right,
        transfer,
        other,
        depth_matrix,
        left_operand(forward),
        left_operand(column_inverse(positions[16:48])),
        right_operand(depth_inverse(depth) * scale),
    )


def halos(block):
    def ring(axis, step):
        count = lax.axis_size(axis)
        return [(i, (i + step) % count) for i in range(count)]

    block, last, first = split(block)
    above = lax.ppermute(last, "px", ring("px", 1))
    below = lax.ppermute(first, "px", ring("px", -1))
    ends, starts = edges(block, above, below)
    left = lax.ppermute(ends, "py", ring("py", 1))
    right = lax.ppermute(starts, "py", ring("py", -1))
    return block, above, below, left, right


def variation(pieces):
    volume, above, below, left, right = pieces
    row_count, col_count, _ = volume.shape
    row_whole = row_count * lax.axis_size("px")
    col_whole = col_count * lax.axis_size("py")
    padded = jnp.concatenate(
        [
            left[15:49, 15:],
            jnp.concatenate([above[15:], volume, below[:1]], 0),
            right[15:49, :1],
        ],
        1,
    )
    region = padded[:-1, :-1]
    slope_rows = padded[1:, :-1] - region
    slope_cols = padded[:-1, 1:] - region
    row_global = lax.axis_index("px") * row_count - 1 + jnp.arange(row_count + 1)
    col_global = lax.axis_index("py") * col_count - 1 + jnp.arange(col_count + 1)
    row_valid = ((row_global >= 0) & (row_global <= row_whole - 2))[:, None, None]
    col_valid = ((col_global >= 0) & (col_global <= col_whole - 2))[None, :, None]
    slope_rows = jnp.where(row_valid, slope_rows, 0.0)
    slope_cols = jnp.where(col_valid, slope_cols, 0.0)
    slope_depth = jnp.concatenate(
        [region[:, :, 1:] - region[:, :, :-1], jnp.zeros_like(region[:, :, :1])], 2
    )
    factor = lax.rsqrt(
        slope_rows * slope_rows
        + slope_cols * slope_cols
        + slope_depth * slope_depth
        + smoothing * smoothing
    )
    flux_rows, flux_cols = slope_rows * factor, slope_cols * factor
    flux_depth = (slope_depth * factor)[1:, 1:]
    flux_depth = flux_depth - jnp.concatenate(
        [jnp.zeros_like(flux_depth[:, :, :1]), flux_depth[:, :, :-1]], 2
    )
    return (
        flux_rows[1:, 1:]
        - flux_rows[:-1, 1:]
        + (flux_cols[1:, 1:] - flux_cols[1:, :-1])
        + flux_depth
    )


def shards(estimate, observed, psf):
    transfer = transfer_function(psf, estimate.shape[2])
    pieces = halos(estimate)
    quotient = convolve(pieces, transfer, observed, False)
    scaled = pieces[0] / (1.0 - penalty_weight * variation(pieces))
    return convolve(halos(quotient), transfer, scaled, True)


def solution(mesh):
    placed = (P("px", "py", None), P("px", "py", None), P())
    return jax.shard_map(
        shards, mesh=mesh, in_specs=placed, out_specs=P("px", "py", None), check_vma=False
    )
```

```python
import functools
import math

import jax
import jax.numpy as jnp
import ml_dtypes
import numpy as np
from jax import lax
from jax.experimental import pallas as pl
from jax.experimental.pallas import tpu as pltpu
from jax.sharding import PartitionSpec as P

penalty_weight = 0.1
smoothing = 0.1

WINDOW = 64
PLANES = 34
ROOT = math.sqrt(0.5)


def two_part(matrix):
    high = matrix.astype(ml_dtypes.bfloat16)
    low = (matrix - high.astype(np.float64)).astype(ml_dtypes.bfloat16)
    return high, low


def right_operand(matrix):
    high, low = two_part(matrix)
    return np.block([[high, low], [high, np.zeros_like(high)]])


def left_operand(matrix):
    high, low = two_part(matrix)
    return np.block([[high, high], [low, np.zeros_like(high)]])


def depth_forward(positions, depth):
    half = depth // 2
    turns = 2.0 * np.pi / depth
    real = np.cos(turns * np.outer(positions, np.arange(half + 1)))
    imag = -np.sin(turns * np.outer(positions, np.arange(1, half)))
    return np.concatenate([real, imag], 1)


def depth_inverse(depth):
    half = depth // 2
    turns = 2.0 * np.pi / depth
    positions = np.arange(depth)
    weight = np.full(half + 1, 2.0)
    weight[0] = weight[half] = 1.0
    real = weight[:, None] * np.cos(turns * np.outer(np.arange(half + 1), positions))
    imag = -2.0 * np.sin(turns * np.outer(np.arange(1, half), positions))
    return np.concatenate([real, imag], 0)


def column_forward(positions):
    angles = 2.0 * np.pi / WINDOW * np.outer(np.arange(WINDOW), positions)
    cosine, sine = np.cos(angles), np.sin(angles)
    return np.block([[cosine, sine], [-sine, cosine]])


def column_inverse(positions):
    angles = 2.0 * np.pi / WINDOW * np.outer(positions, np.arange(WINDOW))
    cosine, sine = np.cos(angles), np.sin(angles)
    return np.block([[cosine, -sine], [sine, cosine]])


def add(a, b):
    return (a[0] + b[0], a[1] + b[1])


def sub(a, b):
    return (a[0] - b[0], a[1] - b[1])


def turn(a, eighths):
    real, imag = a
    eighths %= 8
    if eighths == 0:
        return a
    if eighths == 2:
        return (-imag, real)
    if eighths == 4:
        return (-real, -imag)
    if eighths == 6:
        return (imag, -real)
    total, gap = (real + imag) * ROOT, (real - imag) * ROOT
    if eighths == 1:
        return (gap, total)
    if eighths == 3:
        return (-total, gap)
    if eighths == 5:
        return (-gap, -total)
    return (total, -gap)


def twiddle(a, power, sign):
    angle = sign * 2.0 * math.pi * power / WINDOW
    cosine, sine = math.cos(angle), math.sin(angle)
    if power == 0:
        return a
    real, imag = a
    return (real * cosine - imag * sine, real * sine + imag * cosine)


def complex_eight(values, sign):
    if len(values) == 1:
        return values
    count = len(values)
    even = complex_eight(values[0::2], sign)
    odd = complex_eight(values[1::2], sign)
    odd = [turn(value, sign * k * (8 // count)) for k, value in enumerate(odd)]
    return [add(e, o) for e, o in zip(even, odd)] + [sub(e, o) for e, o in zip(even, odd)]


def real_eight(a):
    s04, d04, s26, d26 = a[0] + a[4], a[0] - a[4], a[2] + a[6], a[2] - a[6]
    s15, d15, s37, d37 = a[1] + a[5], a[1] - a[5], a[3] + a[7], a[3] - a[7]
    even, odd = s04 + s26, s15 + s37
    gap, total = (d15 - d37) * ROOT, (d15 + d37) * ROOT
    return (
        even + odd,
        (d04 + gap, -d26 - total),
        (s04 - s26, s37 - s15),
        (d04 - gap, d26 - total),
        even - odd,
    )


def rows_forward(load, store, zero):
    first = [real_eight([load(8 * x1 + x0) for x1 in range(8)]) for x0 in range(8)]
    ends = real_eight([f[0] for f in first])
    store(0, ends[0], zero)
    for k0 in (1, 2, 3):
        store(k0, *ends[k0])
    store(4, ends[4], zero)
    plane = 5
    for k1 in (1, 2, 3):
        out = complex_eight([twiddle(first[x0][k1], k1 * x0, -1) for x0 in range(8)], -1)
        for value in out:
            store(plane, *value)
            plane += 1
    middle = []
    for x0 in range(8):
        angle = 2.0 * math.pi * 4 * x0 / WINDOW
        middle.append((first[x0][4] * math.cos(angle), first[x0][4] * -math.sin(angle)))
    middle = complex_eight(middle, -1)
    for k0 in range(4):
        store(plane, *middle[k0])
        plane += 1


def rows_inverse(load, store):
    ends = [load(p) for p in range(5)]
    x0r, x4r = ends[0][0], ends[4][0]
    spectrum = [(x0r, jnp.zeros_like(x0r))] + [ends[k] for k in (1, 2, 3)]
    parts = [[None] * 8 for _ in range(5)]
    (r1, i1), (r2, i2), (r3, i3) = [(2.0 * e[0], 2.0 * e[1]) for e in ends[1:4]]
    del spectrum
    base, flip = x0r + x4r, x0r - x4r
    g13, t13 = r1 - r3, r1 + r3
    h13, u13 = i1 - i3, i1 + i3
    parts[0][0] = base + t13 + r2
    parts[0][4] = base - t13 + r2
    parts[0][2] = base - r2 - h13
    parts[0][6] = base - r2 + h13
    odd_a, odd_b = g13 * ROOT, u13 * ROOT
    parts[0][1] = flip + odd_a - odd_b - i2
    parts[0][5] = flip - odd_a + odd_b - i2
    parts[0][3] = flip - odd_a - odd_b + i2
    parts[0][7] = flip + odd_a + odd_b + i2
    plane = 5
    for k1 in (1, 2, 3):
        values = complex_eight([load(plane + k0) for k0 in range(8)], 1)
        plane += 8
        parts[k1] = [twiddle(values[x0], k1 * x0, 1) for x0 in range(8)]
    half = [load(plane + k0) for k0 in range(4)]
    middle = complex_eight(half + [(half[3 - k][0], -half[3 - k][1]) for k in range(4)], 1)
    for x0 in range(8):
        angle = 2.0 * math.pi * 4 * x0 / WINDOW
        parts[4][x0] = middle[x0][0] * math.cos(angle) - middle[x0][1] * math.sin(angle)
    for x0 in range(8):
        v0, v4 = parts[0][x0], parts[4][x0]
        (a, b), (c, d), (e, f) = parts[1][x0], parts[2][x0], parts[3][x0]
        plus, minus = v0 + v4, v0 - v4
        store(16 + x0, plus + 2.0 * (f - b - c))
        store(24 + x0, minus + 2.0 * (d + ROOT * ((e - f) - (a + b))))
        store(32 + x0, plus + 2.0 * (c - a - e))
        store(40 + x0, minus + 2.0 * (ROOT * ((b - a) + (e + f)) - d))


def parts_of(value):
    high = value.astype(jnp.bfloat16)
    low = (value - high.astype(jnp.float32)).astype(jnp.bfloat16)
    return high, low


def along_depth(rows, matrix):
    high, low = parts_of(rows)
    out = jnp.dot(
        jnp.concatenate([high, low], 1), matrix, preferred_element_type=jnp.float32
    )
    return out[:, :128] + out[:, 128:]


def along_columns(matrix, value):
    high, low = parts_of(value)
    out = jnp.dot(
        matrix, jnp.concatenate([high, low], 0), preferred_element_type=jnp.float32
    )
    half = out.shape[0] // 2
    return out[:half] + out[half:]


def transfer_kernel(psf_ref, depth_ref, column_ref, factors, field, rows):
    size = psf_ref.shape[0]
    for x in range(0, size, 8):
        values = psf_ref[x : x + 8].reshape(8 * size, size)
        field[x : x + 8] = jnp.dot(
            values,
            depth_ref[...],
            precision=lax.Precision.HIGHEST,
            preferred_element_type=jnp.float32,
        ).reshape(8, size, 128)
    zero = jnp.zeros((8, 128), jnp.float32)
    rows[PLANES - 1] = jnp.zeros_like(rows[0])

    def chunk(c, carry):
        here = pl.ds(pl.multiple_of(c * 8, 8), 8)
        there = pl.ds(pl.multiple_of(c * 8 + size, 8), 8)

        def load(x):
            tap = (x + size // 2) % WINDOW
            return field[tap, here, :] if tap < size else zero

        def store(plane, real, imag):
            rows[plane, here, :] = real
            rows[plane, there, :] = imag

        rows_forward(load, store, zero)
        return carry

    lax.fori_loop(0, size // 8, chunk, 0)
    lane = lax.broadcasted_iota(jnp.int32, (1, 128), 1)
    real_lane = lane <= 64
    first_half = lane < 64
    alone = (lane == 0) | (lane == 64)
    for p in range(0, PLANES, 2):
        both = along_columns(column_ref[...], jnp.concatenate([rows[p], rows[p + 1]], 1))
        for k in range(2):
            spectrum = both[:, 128 * k : 128 * (k + 1)]
            other = pltpu.roll(spectrum, 64, 1)
            factors[p + k, :128, :] = jnp.where(real_lane, spectrum, other)
            factors[p + k, 128:, :] = jnp.where(
                alone, 0.0, jnp.where(first_half, -other, spectrum)
            )


def depth_piece(ref, matrix, field, x_from, y_from):
    count, width, lanes = ref.shape
    step = 512 // width
    for x in range(0, count, step):
        values = ref[x : x + step].reshape(step * width, lanes)
        field[x_from + x : x_from + x + step, y_from : y_from + width, :] = along_depth(
            values, matrix
        ).reshape(step, width, lanes)


def row_transforms(field, rows, width):
    zero = jnp.zeros((8, 128), jnp.float32)
    rows[PLANES - 1] = jnp.zeros_like(rows[0])

    def chunk(c, carry):
        here = pl.ds(pl.multiple_of(c * 8, 8), 8)
        there = pl.ds(pl.multiple_of(c * 8 + width, 8), 8)

        def load(x):
            return field[x, here, :]

        def store(plane, real, imag):
            rows[plane, here, :] = real
            rows[plane, there, :] = imag

        rows_forward(load, store, zero)
        return carry

    lax.fori_loop(0, width // 8, chunk, 0)


def edges_kernel(first_ref, last_ref, above_ref, below_ref, ends_ref, starts_ref):
    for i, ref in enumerate((above_ref, first_ref, last_ref, below_ref)):
        ends_ref[16 * i : 16 * i + 16] = ref[:, 16:, :]
        starts_ref[16 * i : 16 * i + 16] = ref[:, :16, :]


def split_kernel(block_ref, first_ref, last_ref, done):
    copies = [
        pltpu.make_async_copy(block_ref.at[pl.ds(16 * i, 16)], ref, done.at[i])
        for i, ref in enumerate((first_ref, last_ref))
    ]
    for copy in copies:
        copy.start()
    for copy in copies:
        copy.wait()


def columns_kernel(count, *refs):
    pieces, (depth_ref, rows_ref, field) = refs[:count], refs[count:]
    matrix = depth_ref[...]
    at = 0
    for ref in pieces:
        depth_piece(ref, matrix, field, at, 0)
        at += ref.shape[0]
    row_transforms(field, rows_ref, field.shape[1])


def convolve_kernel(
    adjoint,
    inner_ref,
    left_ref,
    right_ref,
    transfer_ref,
    other_ref,
    depth_ref,
    column_ref,
    column_back_ref,
    depth_back_ref,
    *out_refs_and_scratch,
):
    *out_refs, right_field, rows, spectra, back, field = out_refs_and_scratch
    depth_piece(right_ref, depth_ref[...], right_field, 0, 0)
    row_transforms(right_field, rows, 16)

    for p in range(0, PLANES, 2):
        spectrum = along_columns(
            column_ref[...],
            jnp.concatenate(
                [
                    jnp.concatenate([inner_ref[k], left_ref[k], rows[k]], 0)
                    for k in (p, p + 1)
                ],
                1,
            ),
        )
        spectra[p] = spectrum[:, :128]
        spectra[p + 1] = spectrum[:, 128:]

    for p in range(0, PLANES, 2):
        weighted = []
        for k in range(2):
            own = spectra[p + k]
            partner = pltpu.roll(own, 64, 1)
            a, b = own[:64], own[64:]
            c, d = partner[:64], partner[64:]
            fr, fi = transfer_ref[p + k, 0:64, :], transfer_ref[p + k, 64:128, :]
            gr, gi = transfer_ref[p + k, 128:192, :], transfer_ref[p + k, 192:256, :]
            if adjoint:
                real = (a * fr + b * fi) - (c * gr + d * gi)
                imag = (b * fr - a * fi) - (d * gr - c * gi)
            else:
                real = (a * fr - b * fi) + (c * gr - d * gi)
                imag = (b * fr + a * fi) + (d * gr + c * gi)
            weighted.append(jnp.concatenate([real, imag], 0))
        result = along_columns(column_back_ref[...], jnp.concatenate(weighted, 1))
        back[p] = result[:, :128]
        back[p + 1] = result[:, 128:]

    def chunk_back(c, carry):
        here = pl.ds(pl.multiple_of(c * 8, 8), 8)
        there = pl.ds(pl.multiple_of(c * 8 + 32, 8), 8)

        def load(plane):
            return back[plane, here, :], back[plane, there, :]

        def store(x, value):
            field[x - 16, here, :] = value

        rows_inverse(load, store)
        return carry

    lax.fori_loop(0, 4, chunk_back, 0)

    matrix = depth_back_ref[...]
    for x in range(0, 32, 16):
        values = field[x : 16 + x].reshape(512, 128)
        result = along_depth(values, matrix).reshape(16, 32, 128)
        if adjoint:
            out_refs[0][x : x + 16] = other_ref[x : x + 16] * result
        else:
            out_refs[x // 16][...] = other_ref[x : x + 16] / result


def vmem(count):
    return [pl.BlockSpec(memory_space=pltpu.VMEM)] * count


def transfer_function(psf, depth):
    size = psf.shape[0]
    offsets = np.arange(size) - size // 2
    return pl.pallas_call(
        transfer_kernel,
        out_shape=jax.ShapeDtypeStruct((PLANES, 256, depth), jnp.float32),
        out_specs=vmem(1)[0],
        scratch_shapes=[
            pltpu.VMEM((size, size, depth), jnp.float32),
            pltpu.VMEM((PLANES, 2 * size, depth), jnp.float32),
        ],
        compiler_params=pltpu.CompilerParams(vmem_limit_bytes=8 * 2**20),
        name="transfer",
    )(
        psf,
        jnp.asarray(depth_forward(offsets, depth), jnp.float32),
        left_operand(column_forward(offsets)),
    )


def edges(first, last, above, below):
    shape = jax.ShapeDtypeStruct((WINDOW, 16, first.shape[2]), jnp.float32)
    return pl.pallas_call(
        edges_kernel,
        out_shape=(shape, shape),
        in_specs=vmem(4),
        out_specs=tuple(vmem(2)),
        compiler_params=pltpu.CompilerParams(vmem_limit_bytes=2 * 2**20),
        name="edges",
    )(first, last, above, below)


def split(block):
    shape = jax.ShapeDtypeStruct((16,) + block.shape[1:], jnp.float32)
    return pl.pallas_call(
        split_kernel,
        out_shape=(shape, shape),
        in_specs=[pl.BlockSpec(memory_space=pltpu.HBM)],
        out_specs=tuple(vmem(2)),
        scratch_shapes=[pltpu.SemaphoreType.DMA((2,))],
        compiler_params=pltpu.CompilerParams(vmem_limit_bytes=2**20),
        name="split",
    )(block)


def columns(pieces, depth_matrix, name):
    _, width, depth = pieces[0].shape
    return pl.pallas_call(
        functools.partial(columns_kernel, len(pieces)),
        out_shape=jax.ShapeDtypeStruct((PLANES, 2 * width, depth), jnp.float32),
        in_specs=vmem(len(pieces) + 1),
        out_specs=vmem(1)[0],
        scratch_shapes=[pltpu.VMEM((WINDOW, width, depth), jnp.float32)],
        compiler_params=pltpu.CompilerParams(vmem_limit_bytes=8 * 2**20),
        name=name,
    )(*pieces, depth_matrix)


def convolve(pieces, transfer, other, adjoint):
    first, last, above, below, left, right = pieces
    depth = other.shape[2]
    positions = np.arange(WINDOW)
    scale = 1.0 / (WINDOW * WINDOW * depth)
    depth_matrix = right_operand(depth_forward(np.arange(depth), depth))
    inner = columns((above, first, last, below), depth_matrix, "inner")
    left = columns((left,), depth_matrix, "left")
    forward = np.concatenate(
        [
            column_forward(positions[16:48]),
            column_forward(positions[:16]),
            column_forward(positions[48:]),
        ],
        1,
    )
    whole = jax.ShapeDtypeStruct(other.shape, jnp.float32)
    half = jax.ShapeDtypeStruct((16,) + other.shape[1:], jnp.float32)
    return pl.pallas_call(
        functools.partial(convolve_kernel, adjoint),
        out_shape=whole if adjoint else (half, half),
        in_specs=vmem(9),
        out_specs=vmem(1)[0] if adjoint else tuple(vmem(2)),
        scratch_shapes=[
            pltpu.VMEM((WINDOW, 16, depth), jnp.float32),
            pltpu.VMEM((PLANES, 32, depth), jnp.float32),
            pltpu.VMEM((PLANES, 2 * WINDOW, depth), jnp.float32),
            pltpu.VMEM((PLANES, WINDOW, depth), jnp.float32),
            pltpu.VMEM((32, 32, depth), jnp.float32),
        ],
        compiler_params=pltpu.CompilerParams(vmem_limit_bytes=20 * 2**20),
        name="correlate" if adjoint else "convolve",
    )(
        inner,
        left,
        right,
        transfer,
        other,
        depth_matrix,
        left_operand(forward),
        left_operand(column_inverse(positions[16:48])),
        right_operand(depth_inverse(depth) * scale),
    )


def halos(first, last):
    def ring(axis, step):
        count = lax.axis_size(axis)
        return [(i, (i + step) % count) for i in range(count)]

    above = lax.ppermute(last, "px", ring("px", 1))
    below = lax.ppermute(first, "px", ring("px", -1))
    ends, starts = edges(first, last, above, below)
    left = lax.ppermute(ends, "py", ring("py", 1))
    right = lax.ppermute(starts, "py", ring("py", -1))
    return first, last, above, below, left, right


def variation(volume, pieces):
    _, _, above, below, left, right = pieces
    row_count, col_count, _ = volume.shape
    row_whole = row_count * lax.axis_size("px")
    col_whole = col_count * lax.axis_size("py")
    padded = jnp.concatenate(
        [
            left[15:49, 15:],
            jnp.concatenate([above[15:], volume, below[:1]], 0),
            right[15:49, :1],
        ],
        1,
    )
    region = padded[:-1, :-1]
    slope_rows = padded[1:, :-1] - region
    slope_cols = padded[:-1, 1:] - region
    row_global = lax.axis_index("px") * row_count - 1 + jnp.arange(row_count + 1)
    col_global = lax.axis_index("py") * col_count - 1 + jnp.arange(col_count + 1)
    row_valid = ((row_global >= 0) & (row_global <= row_whole - 2))[:, None, None]
    col_valid = ((col_global >= 0) & (col_global <= col_whole - 2))[None, :, None]
    slope_rows = jnp.where(row_valid, slope_rows, 0.0)
    slope_cols = jnp.where(col_valid, slope_cols, 0.0)
    slope_depth = jnp.concatenate(
        [region[:, :, 1:] - region[:, :, :-1], jnp.zeros_like(region[:, :, :1])], 2
    )
    factor = lax.rsqrt(
        slope_rows * slope_rows
        + slope_cols * slope_cols
        + slope_depth * slope_depth
        + smoothing * smoothing
    )
    flux_rows, flux_cols = slope_rows * factor, slope_cols * factor
    flux_depth = (slope_depth * factor)[1:, 1:]
    flux_depth = flux_depth - jnp.concatenate(
        [jnp.zeros_like(flux_depth[:, :, :1]), flux_depth[:, :, :-1]], 2
    )
    return (
        flux_rows[1:, 1:]
        - flux_rows[:-1, 1:]
        + (flux_cols[1:, 1:] - flux_cols[1:, :-1])
        + flux_depth
    )


def shards(estimate, observed, psf):
    transfer = transfer_function(psf, estimate.shape[2])
    pieces = halos(*split(estimate))
    quotient = convolve(pieces, transfer, observed, False)
    scaled = estimate / (1.0 - penalty_weight * variation(estimate, pieces))
    return convolve(halos(*quotient), transfer, scaled, True)


def solution(mesh):
    placed = (P("px", "py", None), P("px", "py", None), P())
    return jax.shard_map(
        shards, mesh=mesh, in_specs=placed, out_specs=P("px", "py", None), check_vma=False
    )
```

```python
import functools
import math

import jax
import jax.numpy as jnp
import ml_dtypes
import numpy as np
from jax import lax
from jax.experimental import pallas as pl
from jax.experimental.pallas import tpu as pltpu
from jax.sharding import PartitionSpec as P

penalty_weight = 0.1
smoothing = 0.1

WINDOW = 64
PLANES = 34
ROOT = math.sqrt(0.5)


def two_part(matrix):
    high = matrix.astype(ml_dtypes.bfloat16)
    low = (matrix - high.astype(np.float64)).astype(ml_dtypes.bfloat16)
    return high, low


def right_operand(matrix):
    high, low = two_part(matrix)
    return np.block([[high, low], [high, np.zeros_like(high)]])


def left_operand(matrix):
    high, low = two_part(matrix)
    return np.block([[high, high], [low, np.zeros_like(high)]])


def depth_forward(positions, depth):
    half = depth // 2
    turns = 2.0 * np.pi / depth
    real = np.cos(turns * np.outer(positions, np.arange(half + 1)))
    imag = -np.sin(turns * np.outer(positions, np.arange(1, half)))
    return np.concatenate([real, imag], 1)


def depth_inverse(depth):
    half = depth // 2
    turns = 2.0 * np.pi / depth
    positions = np.arange(depth)
    weight = np.full(half + 1, 2.0)
    weight[0] = weight[half] = 1.0
    real = weight[:, None] * np.cos(turns * np.outer(np.arange(half + 1), positions))
    imag = -2.0 * np.sin(turns * np.outer(np.arange(1, half), positions))
    return np.concatenate([real, imag], 0)


def column_forward(positions):
    angles = 2.0 * np.pi / WINDOW * np.outer(np.arange(WINDOW), positions)
    cosine, sine = np.cos(angles), np.sin(angles)
    return np.block([[cosine, sine], [-sine, cosine]])


def column_inverse(positions):
    angles = 2.0 * np.pi / WINDOW * np.outer(positions, np.arange(WINDOW))
    cosine, sine = np.cos(angles), np.sin(angles)
    return np.block([[cosine, -sine], [sine, cosine]])


def add(a, b):
    return (a[0] + b[0], a[1] + b[1])


def sub(a, b):
    return (a[0] - b[0], a[1] - b[1])


def turn(a, eighths):
    real, imag = a
    eighths %= 8
    if eighths == 0:
        return a
    if eighths == 2:
        return (-imag, real)
    if eighths == 4:
        return (-real, -imag)
    if eighths == 6:
        return (imag, -real)
    total, gap = (real + imag) * ROOT, (real - imag) * ROOT
    if eighths == 1:
        return (gap, total)
    if eighths == 3:
        return (-total, gap)
    if eighths == 5:
        return (-gap, -total)
    return (total, -gap)


def twiddle(a, power, sign):
    angle = sign * 2.0 * math.pi * power / WINDOW
    cosine, sine = math.cos(angle), math.sin(angle)
    if power == 0:
        return a
    real, imag = a
    return (real * cosine - imag * sine, real * sine + imag * cosine)


def complex_eight(values, sign):
    if len(values) == 1:
        return values
    count = len(values)
    even = complex_eight(values[0::2], sign)
    odd = complex_eight(values[1::2], sign)
    odd = [turn(value, sign * k * (8 // count)) for k, value in enumerate(odd)]
    return [add(e, o) for e, o in zip(even, odd)] + [sub(e, o) for e, o in zip(even, odd)]


def real_eight(a):
    s04, d04, s26, d26 = a[0] + a[4], a[0] - a[4], a[2] + a[6], a[2] - a[6]
    s15, d15, s37, d37 = a[1] + a[5], a[1] - a[5], a[3] + a[7], a[3] - a[7]
    even, odd = s04 + s26, s15 + s37
    gap, total = (d15 - d37) * ROOT, (d15 + d37) * ROOT
    return (
        even + odd,
        (d04 + gap, -d26 - total),
        (s04 - s26, s37 - s15),
        (d04 - gap, d26 - total),
        even - odd,
    )


def rows_forward(load, store, zero):
    first = [real_eight([load(8 * x1 + x0) for x1 in range(8)]) for x0 in range(8)]
    ends = real_eight([f[0] for f in first])
    store(0, ends[0], zero)
    for k0 in (1, 2, 3):
        store(k0, *ends[k0])
    store(4, ends[4], zero)
    plane = 5
    for k1 in (1, 2, 3):
        out = complex_eight([twiddle(first[x0][k1], k1 * x0, -1) for x0 in range(8)], -1)
        for value in out:
            store(plane, *value)
            plane += 1
    middle = []
    for x0 in range(8):
        angle = 2.0 * math.pi * 4 * x0 / WINDOW
        middle.append((first[x0][4] * math.cos(angle), first[x0][4] * -math.sin(angle)))
    middle = complex_eight(middle, -1)
    for k0 in range(4):
        store(plane, *middle[k0])
        plane += 1


def rows_inverse(load, store):
    ends = [load(p) for p in range(5)]
    x0r, x4r = ends[0][0], ends[4][0]
    spectrum = [(x0r, jnp.zeros_like(x0r))] + [ends[k] for k in (1, 2, 3)]
    parts = [[None] * 8 for _ in range(5)]
    (r1, i1), (r2, i2), (r3, i3) = [(2.0 * e[0], 2.0 * e[1]) for e in ends[1:4]]
    del spectrum
    base, flip = x0r + x4r, x0r - x4r
    g13, t13 = r1 - r3, r1 + r3
    h13, u13 = i1 - i3, i1 + i3
    parts[0][0] = base + t13 + r2
    parts[0][4] = base - t13 + r2
    parts[0][2] = base - r2 - h13
    parts[0][6] = base - r2 + h13
    odd_a, odd_b = g13 * ROOT, u13 * ROOT
    parts[0][1] = flip + odd_a - odd_b - i2
    parts[0][5] = flip - odd_a + odd_b - i2
    parts[0][3] = flip - odd_a - odd_b + i2
    parts[0][7] = flip + odd_a + odd_b + i2
    plane = 5
    for k1 in (1, 2, 3):
        values = complex_eight([load(plane + k0) for k0 in range(8)], 1)
        plane += 8
        parts[k1] = [twiddle(values[x0], k1 * x0, 1) for x0 in range(8)]
    half = [load(plane + k0) for k0 in range(4)]
    middle = complex_eight(half + [(half[3 - k][0], -half[3 - k][1]) for k in range(4)], 1)
    for x0 in range(8):
        angle = 2.0 * math.pi * 4 * x0 / WINDOW
        parts[4][x0] = middle[x0][0] * math.cos(angle) - middle[x0][1] * math.sin(angle)
    for x0 in range(8):
        v0, v4 = parts[0][x0], parts[4][x0]
        (a, b), (c, d), (e, f) = parts[1][x0], parts[2][x0], parts[3][x0]
        plus, minus = v0 + v4, v0 - v4
        store(16 + x0, plus + 2.0 * (f - b - c))
        store(24 + x0, minus + 2.0 * (d + ROOT * ((e - f) - (a + b))))
        store(32 + x0, plus + 2.0 * (c - a - e))
        store(40 + x0, minus + 2.0 * (ROOT * ((b - a) + (e + f)) - d))


def parts_of(value):
    high = value.astype(jnp.bfloat16)
    low = (value - high.astype(jnp.float32)).astype(jnp.bfloat16)
    return high, low


def along_depth(rows, matrix):
    high, low = parts_of(rows)
    out = jnp.dot(
        jnp.concatenate([high, low], 1), matrix, preferred_element_type=jnp.float32
    )
    return out[:, :128] + out[:, 128:]


def along_columns(matrix, value):
    high, low = parts_of(value)
    out = jnp.dot(
        matrix, jnp.concatenate([high, low], 0), preferred_element_type=jnp.float32
    )
    half = out.shape[0] // 2
    return out[:half] + out[half:]


def transfer_kernel(psf_ref, depth_ref, column_ref, factors, field, rows):
    size = psf_ref.shape[0]
    for x in range(0, size, 8):
        values = psf_ref[x : x + 8].reshape(8 * size, size)
        field[x : x + 8] = jnp.dot(
            values,
            depth_ref[...],
            precision=lax.Precision.HIGHEST,
            preferred_element_type=jnp.float32,
        ).reshape(8, size, 128)
    zero = jnp.zeros((8, 128), jnp.float32)
    rows[PLANES - 1] = jnp.zeros_like(rows[0])

    def chunk(c, carry):
        here = pl.ds(pl.multiple_of(c * 8, 8), 8)
        there = pl.ds(pl.multiple_of(c * 8 + size, 8), 8)

        def load(x):
            tap = (x + size // 2) % WINDOW
            return field[tap, here, :] if tap < size else zero

        def store(plane, real, imag):
            rows[plane, here, :] = real
            rows[plane, there, :] = imag

        rows_forward(load, store, zero)
        return carry

    lax.fori_loop(0, size // 8, chunk, 0)
    lane = lax.broadcasted_iota(jnp.int32, (1, 128), 1)
    real_lane = lane <= 64
    first_half = lane < 64
    alone = (lane == 0) | (lane == 64)
    for p in range(0, PLANES, 2):
        both = along_columns(column_ref[...], jnp.concatenate([rows[p], rows[p + 1]], 1))
        for k in range(2):
            spectrum = both[:, 128 * k : 128 * (k + 1)]
            other = pltpu.roll(spectrum, 64, 1)
            factors[p + k, :128, :] = jnp.where(real_lane, spectrum, other)
            factors[p + k, 128:, :] = jnp.where(
                alone, 0.0, jnp.where(first_half, -other, spectrum)
            )


def depth_piece(ref, matrix, field, x_from, y_from):
    count, width, lanes = ref.shape
    step = 512 // width
    for x in range(0, count, step):
        values = ref[x : x + step].reshape(step * width, lanes)
        field[x_from + x : x_from + x + step, y_from : y_from + width, :] = along_depth(
            values, matrix
        ).reshape(step, width, lanes)


def row_transforms(field, rows, width):
    zero = jnp.zeros((8, 128), jnp.float32)
    rows[PLANES - 1] = jnp.zeros_like(rows[0])

    def chunk(c, carry):
        here = pl.ds(pl.multiple_of(c * 8, 8), 8)
        there = pl.ds(pl.multiple_of(c * 8 + width, 8), 8)

        def load(x):
            return field[x, here, :]

        def store(plane, real, imag):
            rows[plane, here, :] = real
            rows[plane, there, :] = imag

        rows_forward(load, store, zero)
        return carry

    lax.fori_loop(0, width // 8, chunk, 0)


def edges_kernel(first_ref, last_ref, above_ref, below_ref, ends_ref, starts_ref):
    for i, ref in enumerate((above_ref, first_ref, last_ref, below_ref)):
        ends_ref[16 * i : 16 * i + 16] = ref[:, 16:, :]
        starts_ref[16 * i : 16 * i + 16] = ref[:, :16, :]


def split_kernel(block_ref, first_ref, last_ref, done):
    copies = [
        pltpu.make_async_copy(block_ref.at[pl.ds(16 * i, 16)], ref, done.at[i])
        for i, ref in enumerate((first_ref, last_ref))
    ]
    for copy in copies:
        copy.start()
    for copy in copies:
        copy.wait()


def columns_kernel(count, *refs):
    pieces, (depth_ref, rows_ref, field) = refs[:count], refs[count:]
    matrix = depth_ref[...]
    at = 0
    for ref in pieces:
        depth_piece(ref, matrix, field, at, 0)
        at += ref.shape[0]
    row_transforms(field, rows_ref, field.shape[1])


def convolve_kernel(
    adjoint,
    inner_ref,
    left_ref,
    right_ref,
    transfer_ref,
    other_ref,
    depth_ref,
    column_ref,
    column_back_ref,
    depth_back_ref,
    *out_refs_and_scratch,
):
    *out_refs, right_field, rows, spectra, back, field = out_refs_and_scratch
    depth_piece(right_ref, depth_ref[...], right_field, 0, 0)
    row_transforms(right_field, rows, 16)

    for p in range(0, PLANES, 2):
        spectrum = along_columns(
            column_ref[...],
            jnp.concatenate(
                [
                    jnp.concatenate([inner_ref[k], left_ref[k], rows[k]], 0)
                    for k in (p, p + 1)
                ],
                1,
            ),
        )
        spectra[p] = spectrum[:, :128]
        spectra[p + 1] = spectrum[:, 128:]

    for p in range(0, PLANES, 2):
        weighted = []
        for k in range(2):
            own = spectra[p + k]
            partner = pltpu.roll(own, 64, 1)
            a, b = own[:64], own[64:]
            c, d = partner[:64], partner[64:]
            fr, fi = transfer_ref[p + k, 0:64, :], transfer_ref[p + k, 64:128, :]
            gr, gi = transfer_ref[p + k, 128:192, :], transfer_ref[p + k, 192:256, :]
            if adjoint:
                real = (a * fr + b * fi) - (c * gr + d * gi)
                imag = (b * fr - a * fi) - (d * gr - c * gi)
            else:
                real = (a * fr - b * fi) + (c * gr - d * gi)
                imag = (b * fr + a * fi) + (d * gr + c * gi)
            weighted.append(jnp.concatenate([real, imag], 0))
        result = along_columns(column_back_ref[...], jnp.concatenate(weighted, 1))
        back[p] = result[:, :128]
        back[p + 1] = result[:, 128:]

    def chunk_back(c, carry):
        here = pl.ds(pl.multiple_of(c * 8, 8), 8)
        there = pl.ds(pl.multiple_of(c * 8 + 32, 8), 8)

        def load(plane):
            return back[plane, here, :], back[plane, there, :]

        def store(x, value):
            field[x - 16, here, :] = value

        rows_inverse(load, store)
        return carry

    lax.fori_loop(0, 4, chunk_back, 0)

    matrix = depth_back_ref[...]
    for x in range(0, 32, 16):
        values = field[x : 16 + x].reshape(512, 128)
        result = along_depth(values, matrix).reshape(16, 32, 128)
        if adjoint:
            out_refs[0][x : x + 16] = other_ref[x : x + 16] * result
        else:
            out_refs[x // 16][...] = other_ref[x : x + 16] / result


def vmem(count):
    return [pl.BlockSpec(memory_space=pltpu.VMEM)] * count


def transfer_function(psf, depth):
    size = psf.shape[0]
    offsets = np.arange(size) - size // 2
    return pl.pallas_call(
        transfer_kernel,
        out_shape=jax.ShapeDtypeStruct((PLANES, 256, depth), jnp.float32),
        out_specs=vmem(1)[0],
        scratch_shapes=[
            pltpu.VMEM((size, size, depth), jnp.float32),
            pltpu.VMEM((PLANES, 2 * size, depth), jnp.float32),
        ],
        compiler_params=pltpu.CompilerParams(vmem_limit_bytes=8 * 2**20),
        name="transfer",
    )(
        psf,
        jnp.asarray(depth_forward(offsets, depth), jnp.float32),
        left_operand(column_forward(offsets)),
    )


def edges(first, last, above, below):
    shape = jax.ShapeDtypeStruct((WINDOW, 16, first.shape[2]), jnp.float32)
    return pl.pallas_call(
        edges_kernel,
        out_shape=(shape, shape),
        in_specs=vmem(4),
        out_specs=tuple(vmem(2)),
        compiler_params=pltpu.CompilerParams(vmem_limit_bytes=2 * 2**20),
        name="edges",
    )(first, last, above, below)


def split(block):
    shape = jax.ShapeDtypeStruct((16,) + block.shape[1:], jnp.float32)
    return pl.pallas_call(
        split_kernel,
        out_shape=(shape, shape),
        in_specs=[pl.BlockSpec(memory_space=pltpu.HBM)],
        out_specs=tuple(vmem(2)),
        scratch_shapes=[pltpu.SemaphoreType.DMA((2,))],
        compiler_params=pltpu.CompilerParams(vmem_limit_bytes=2**20),
        name="split",
    )(block)


def columns(pieces, depth_matrix, name):
    _, width, depth = pieces[0].shape
    return pl.pallas_call(
        functools.partial(columns_kernel, len(pieces)),
        out_shape=jax.ShapeDtypeStruct((PLANES, 2 * width, depth), jnp.float32),
        in_specs=vmem(len(pieces) + 1),
        out_specs=vmem(1)[0],
        scratch_shapes=[pltpu.VMEM((WINDOW, width, depth), jnp.float32)],
        compiler_params=pltpu.CompilerParams(vmem_limit_bytes=8 * 2**20),
        name=name,
    )(*pieces, depth_matrix)


def convolve(pieces, transfer, other, adjoint):
    first, last, above, below, left, right = pieces
    depth = other.shape[2]
    positions = np.arange(WINDOW)
    scale = 1.0 / (WINDOW * WINDOW * depth)
    depth_matrix = right_operand(depth_forward(np.arange(depth), depth))
    inner = columns((above, first, last, below), depth_matrix, "inner")
    left = columns((left,), depth_matrix, "left")
    forward = np.concatenate(
        [
            column_forward(positions[16:48]),
            column_forward(positions[:16]),
            column_forward(positions[48:]),
        ],
        1,
    )
    whole = jax.ShapeDtypeStruct(other.shape, jnp.float32)
    half = jax.ShapeDtypeStruct((16,) + other.shape[1:], jnp.float32)
    return pl.pallas_call(
        functools.partial(convolve_kernel, adjoint),
        out_shape=whole if adjoint else (half, half),
        in_specs=vmem(9),
        out_specs=vmem(1)[0] if adjoint else tuple(vmem(2)),
        scratch_shapes=[
            pltpu.VMEM((WINDOW, 16, depth), jnp.float32),
            pltpu.VMEM((PLANES, 32, depth), jnp.float32),
            pltpu.VMEM((PLANES, 2 * WINDOW, depth), jnp.float32),
            pltpu.VMEM((PLANES, WINDOW, depth), jnp.float32),
            pltpu.VMEM((32, 32, depth), jnp.float32),
        ],
        compiler_params=pltpu.CompilerParams(vmem_limit_bytes=20 * 2**20),
        name="correlate" if adjoint else "convolve",
    )(
        inner,
        left,
        right,
        transfer,
        other,
        depth_matrix,
        left_operand(forward),
        left_operand(column_inverse(positions[16:48])),
        right_operand(depth_inverse(depth) * scale),
    )


def halos(first, last):
    def ring(axis, step):
        count = lax.axis_size(axis)
        return [(i, (i + step) % count) for i in range(count)]

    above = lax.ppermute(last, "px", ring("px", 1))
    below = lax.ppermute(first, "px", ring("px", -1))
    ends, starts = edges(first, last, above, below)
    left = lax.ppermute(ends, "py", ring("py", 1))
    right = lax.ppermute(starts, "py", ring("py", -1))
    return first, last, above, below, left, right


def variation(volume, pieces):
    _, _, above, below, left, right = pieces
    row_count, col_count, _ = volume.shape
    row_whole = row_count * lax.axis_size("px")
    col_whole = col_count * lax.axis_size("py")
    padded = jnp.concatenate(
        [
            left[15:49, 15:],
            jnp.concatenate([above[15:], volume, below[:1]], 0),
            right[15:49, :1],
        ],
        1,
    )
    region = padded[:-1, :-1]
    slope_rows = padded[1:, :-1] - region
    slope_cols = padded[:-1, 1:] - region
    row_global = lax.axis_index("px") * row_count - 1 + jnp.arange(row_count + 1)
    col_global = lax.axis_index("py") * col_count - 1 + jnp.arange(col_count + 1)
    row_valid = ((row_global >= 0) & (row_global <= row_whole - 2))[:, None, None]
    col_valid = ((col_global >= 0) & (col_global <= col_whole - 2))[None, :, None]
    slope_rows = jnp.where(row_valid, slope_rows, 0.0)
    slope_cols = jnp.where(col_valid, slope_cols, 0.0)
    slope_depth = jnp.concatenate(
        [region[:, :, 1:] - region[:, :, :-1], jnp.zeros_like(region[:, :, :1])], 2
    )
    factor = lax.rsqrt(
        slope_rows * slope_rows
        + slope_cols * slope_cols
        + slope_depth * slope_depth
        + smoothing * smoothing
    )
    flux_rows, flux_cols = slope_rows * factor, slope_cols * factor
    flux_depth = (slope_depth * factor)[1:, 1:]
    flux_depth = flux_depth - jnp.concatenate(
        [jnp.zeros_like(flux_depth[:, :, :1]), flux_depth[:, :, :-1]], 2
    )
    return (
        flux_rows[1:, 1:]
        - flux_rows[:-1, 1:]
        + (flux_cols[1:, 1:] - flux_cols[1:, :-1])
        + flux_depth
    )


def shards(estimate, observed, psf):
    transfer = transfer_function(psf, estimate.shape[2])
    pieces = halos(*split(estimate))
    quotient = convolve(pieces, transfer, observed, False)
    around, quotient = lax.optimization_barrier((pieces[2:], quotient))
    scaled = estimate / (1.0 - penalty_weight * variation(estimate, pieces[:2] + around))
    return convolve(halos(*quotient), transfer, scaled, True)


def solution(mesh):
    placed = (P("px", "py", None), P("px", "py", None), P())
    return jax.shard_map(
        shards, mesh=mesh, in_specs=placed, out_specs=P("px", "py", None), check_vma=False
    )
```

```python
import functools
import math

import jax
import jax.numpy as jnp
import ml_dtypes
import numpy as np
from jax import lax
from jax.experimental import pallas as pl
from jax.experimental.pallas import tpu as pltpu
from jax.sharding import PartitionSpec as P

penalty_weight = 0.1
smoothing = 0.1

WINDOW = 64
PLANES = 34
ROOT = math.sqrt(0.5)


def two_part(matrix):
    high = matrix.astype(ml_dtypes.bfloat16)
    low = (matrix - high.astype(np.float64)).astype(ml_dtypes.bfloat16)
    return high, low


def right_operand(matrix):
    high, low = two_part(matrix)
    return np.block([[high, low], [high, np.zeros_like(high)]])


def left_operand(matrix):
    high, low = two_part(matrix)
    return np.block([[high, high], [low, np.zeros_like(high)]])


def depth_forward(positions, depth):
    half = depth // 2
    turns = 2.0 * np.pi / depth
    real = np.cos(turns * np.outer(positions, np.arange(half + 1)))
    imag = -np.sin(turns * np.outer(positions, np.arange(1, half)))
    return np.concatenate([real, imag], 1)


def depth_inverse(depth):
    half = depth // 2
    turns = 2.0 * np.pi / depth
    positions = np.arange(depth)
    weight = np.full(half + 1, 2.0)
    weight[0] = weight[half] = 1.0
    real = weight[:, None] * np.cos(turns * np.outer(np.arange(half + 1), positions))
    imag = -2.0 * np.sin(turns * np.outer(np.arange(1, half), positions))
    return np.concatenate([real, imag], 0)


def column_forward(positions):
    angles = 2.0 * np.pi / WINDOW * np.outer(np.arange(WINDOW), positions)
    cosine, sine = np.cos(angles), np.sin(angles)
    return np.block([[cosine, sine], [-sine, cosine]])


def column_inverse(positions):
    angles = 2.0 * np.pi / WINDOW * np.outer(positions, np.arange(WINDOW))
    cosine, sine = np.cos(angles), np.sin(angles)
    return np.block([[cosine, -sine], [sine, cosine]])


def add(a, b):
    return (a[0] + b[0], a[1] + b[1])


def sub(a, b):
    return (a[0] - b[0], a[1] - b[1])


def turn(a, eighths):
    real, imag = a
    eighths %= 8
    if eighths == 0:
        return a
    if eighths == 2:
        return (-imag, real)
    if eighths == 4:
        return (-real, -imag)
    if eighths == 6:
        return (imag, -real)
    total, gap = (real + imag) * ROOT, (real - imag) * ROOT
    if eighths == 1:
        return (gap, total)
    if eighths == 3:
        return (-total, gap)
    if eighths == 5:
        return (-gap, -total)
    return (total, -gap)


def twiddle(a, power, sign):
    angle = sign * 2.0 * math.pi * power / WINDOW
    cosine, sine = math.cos(angle), math.sin(angle)
    if power == 0:
        return a
    real, imag = a
    return (real * cosine - imag * sine, real * sine + imag * cosine)


def complex_eight(values, sign):
    if len(values) == 1:
        return values
    count = len(values)
    even = complex_eight(values[0::2], sign)
    odd = complex_eight(values[1::2], sign)
    odd = [turn(value, sign * k * (8 // count)) for k, value in enumerate(odd)]
    return [add(e, o) for e, o in zip(even, odd)] + [sub(e, o) for e, o in zip(even, odd)]


def real_eight(a):
    s04, d04, s26, d26 = a[0] + a[4], a[0] - a[4], a[2] + a[6], a[2] - a[6]
    s15, d15, s37, d37 = a[1] + a[5], a[1] - a[5], a[3] + a[7], a[3] - a[7]
    even, odd = s04 + s26, s15 + s37
    gap, total = (d15 - d37) * ROOT, (d15 + d37) * ROOT
    return (
        even + odd,
        (d04 + gap, -d26 - total),
        (s04 - s26, s37 - s15),
        (d04 - gap, d26 - total),
        even - odd,
    )


def rows_forward(load, store, zero):
    first = [real_eight([load(8 * x1 + x0) for x1 in range(8)]) for x0 in range(8)]
    ends = real_eight([f[0] for f in first])
    store(0, ends[0], zero)
    for k0 in (1, 2, 3):
        store(k0, *ends[k0])
    store(4, ends[4], zero)
    plane = 5
    for k1 in (1, 2, 3):
        out = complex_eight([twiddle(first[x0][k1], k1 * x0, -1) for x0 in range(8)], -1)
        for value in out:
            store(plane, *value)
            plane += 1
    middle = []
    for x0 in range(8):
        angle = 2.0 * math.pi * 4 * x0 / WINDOW
        middle.append((first[x0][4] * math.cos(angle), first[x0][4] * -math.sin(angle)))
    middle = complex_eight(middle, -1)
    for k0 in range(4):
        store(plane, *middle[k0])
        plane += 1


def rows_inverse(load, store):
    ends = [load(p) for p in range(5)]
    x0r, x4r = ends[0][0], ends[4][0]
    spectrum = [(x0r, jnp.zeros_like(x0r))] + [ends[k] for k in (1, 2, 3)]
    parts = [[None] * 8 for _ in range(5)]
    (r1, i1), (r2, i2), (r3, i3) = [(2.0 * e[0], 2.0 * e[1]) for e in ends[1:4]]
    del spectrum
    base, flip = x0r + x4r, x0r - x4r
    g13, t13 = r1 - r3, r1 + r3
    h13, u13 = i1 - i3, i1 + i3
    parts[0][0] = base + t13 + r2
    parts[0][4] = base - t13 + r2
    parts[0][2] = base - r2 - h13
    parts[0][6] = base - r2 + h13
    odd_a, odd_b = g13 * ROOT, u13 * ROOT
    parts[0][1] = flip + odd_a - odd_b - i2
    parts[0][5] = flip - odd_a + odd_b - i2
    parts[0][3] = flip - odd_a - odd_b + i2
    parts[0][7] = flip + odd_a + odd_b + i2
    plane = 5
    for k1 in (1, 2, 3):
        values = complex_eight([load(plane + k0) for k0 in range(8)], 1)
        plane += 8
        parts[k1] = [twiddle(values[x0], k1 * x0, 1) for x0 in range(8)]
    half = [load(plane + k0) for k0 in range(4)]
    middle = complex_eight(half + [(half[3 - k][0], -half[3 - k][1]) for k in range(4)], 1)
    for x0 in range(8):
        angle = 2.0 * math.pi * 4 * x0 / WINDOW
        parts[4][x0] = middle[x0][0] * math.cos(angle) - middle[x0][1] * math.sin(angle)
    for x0 in range(8):
        v0, v4 = parts[0][x0], parts[4][x0]
        (a, b), (c, d), (e, f) = parts[1][x0], parts[2][x0], parts[3][x0]
        plus, minus = v0 + v4, v0 - v4
        store(16 + x0, plus + 2.0 * (f - b - c))
        store(24 + x0, minus + 2.0 * (d + ROOT * ((e - f) - (a + b))))
        store(32 + x0, plus + 2.0 * (c - a - e))
        store(40 + x0, minus + 2.0 * (ROOT * ((b - a) + (e + f)) - d))


def parts_of(value):
    high = value.astype(jnp.bfloat16)
    low = (value - high.astype(jnp.float32)).astype(jnp.bfloat16)
    return high, low


def along_depth(rows, matrix):
    high, low = parts_of(rows)
    out = jnp.dot(
        jnp.concatenate([high, low], 1), matrix, preferred_element_type=jnp.float32
    )
    return out[:, :128] + out[:, 128:]


def along_columns(matrix, value):
    high, low = parts_of(value)
    out = jnp.dot(
        matrix, jnp.concatenate([high, low], 0), preferred_element_type=jnp.float32
    )
    half = out.shape[0] // 2
    return out[:half] + out[half:]


def transfer_kernel(psf_ref, depth_ref, column_ref, factors, field, rows):
    size = psf_ref.shape[0]
    for x in range(0, size, 8):
        values = psf_ref[x : x + 8].reshape(8 * size, size)
        field[x : x + 8] = jnp.dot(
            values,
            depth_ref[...],
            precision=lax.Precision.HIGHEST,
            preferred_element_type=jnp.float32,
        ).reshape(8, size, 128)
    zero = jnp.zeros((8, 128), jnp.float32)
    rows[PLANES - 1] = jnp.zeros_like(rows[0])

    def chunk(c, carry):
        here = pl.ds(pl.multiple_of(c * 8, 8), 8)
        there = pl.ds(pl.multiple_of(c * 8 + size, 8), 8)

        def load(x):
            tap = (x + size // 2) % WINDOW
            return field[tap, here, :] if tap < size else zero

        def store(plane, real, imag):
            rows[plane, here, :] = real
            rows[plane, there, :] = imag

        rows_forward(load, store, zero)
        return carry

    lax.fori_loop(0, size // 8, chunk, 0)
    lane = lax.broadcasted_iota(jnp.int32, (1, 128), 1)
    real_lane = lane <= 64
    first_half = lane < 64
    alone = (lane == 0) | (lane == 64)
    for p in range(0, PLANES, 2):
        both = along_columns(column_ref[...], jnp.concatenate([rows[p], rows[p + 1]], 1))
        for k in range(2):
            spectrum = both[:, 128 * k : 128 * (k + 1)]
            other = pltpu.roll(spectrum, 64, 1)
            factors[p + k, :128, :] = jnp.where(real_lane, spectrum, other)
            factors[p + k, 128:, :] = jnp.where(
                alone, 0.0, jnp.where(first_half, -other, spectrum)
            )


def depth_piece(ref, matrix, field, x_from, y_from):
    count, width, lanes = ref.shape
    step = 512 // width
    for x in range(0, count, step):
        size = min(step, count - x)
        values = ref[x : x + size].reshape(size * width, lanes)
        field[x_from + x : x_from + x + size, y_from : y_from + width, :] = along_depth(
            values, matrix
        ).reshape(size, width, lanes)


def row_transforms(field, rows, width):
    zero = jnp.zeros((8, 128), jnp.float32)
    rows[PLANES - 1] = jnp.zeros_like(rows[0])

    def chunk(c, carry):
        here = pl.ds(pl.multiple_of(c * 8, 8), 8)
        there = pl.ds(pl.multiple_of(c * 8 + width, 8), 8)

        def load(x):
            return field[x, here, :]

        def store(plane, real, imag):
            rows[plane, here, :] = real
            rows[plane, there, :] = imag

        rows_forward(load, store, zero)
        return carry

    lax.fori_loop(0, width // 8, chunk, 0)


def edge_kernel(side, first_ref, last_ref, above_ref, below_ref, out_ref):
    at = 0
    for ref in (above_ref, first_ref, last_ref, below_ref):
        count = ref.shape[0]
        out_ref[at : at + count] = ref[:, side : side + 16, :]
        at += count
    if at < WINDOW:
        out_ref[at] = jnp.zeros_like(out_ref[0])


def split_kernel(block_ref, first_ref, last_ref, done):
    copies = [
        pltpu.make_async_copy(block_ref.at[pl.ds(16 * i, 16)], ref, done.at[i])
        for i, ref in enumerate((first_ref, last_ref))
    ]
    for copy in copies:
        copy.start()
    for copy in copies:
        copy.wait()


def columns_kernel(count, *refs):
    pieces, (depth_ref, rows_ref, field) = refs[:count], refs[count:]
    matrix = depth_ref[...]
    at = 0
    for ref in pieces:
        depth_piece(ref, matrix, field, at, 0)
        at += ref.shape[0]
    if at < WINDOW:
        field[at] = jnp.zeros_like(field[0])
    row_transforms(field, rows_ref, field.shape[1])


def convolve_kernel(
    adjoint,
    inner_ref,
    left_ref,
    right_ref,
    transfer_ref,
    other_ref,
    depth_ref,
    column_ref,
    column_back_ref,
    depth_back_ref,
    *out_refs_and_scratch,
):
    *out_refs, right_field, rows, spectra, back, field = out_refs_and_scratch
    depth_piece(right_ref, depth_ref[...], right_field, 0, 0)
    row_transforms(right_field, rows, 16)

    for p in range(0, PLANES, 2):
        spectrum = along_columns(
            column_ref[...],
            jnp.concatenate(
                [
                    jnp.concatenate([inner_ref[k], left_ref[k], rows[k]], 0)
                    for k in (p, p + 1)
                ],
                1,
            ),
        )
        spectra[p] = spectrum[:, :128]
        spectra[p + 1] = spectrum[:, 128:]

    for p in range(0, PLANES, 2):
        weighted = []
        for k in range(2):
            own = spectra[p + k]
            partner = pltpu.roll(own, 64, 1)
            a, b = own[:64], own[64:]
            c, d = partner[:64], partner[64:]
            fr, fi = transfer_ref[p + k, 0:64, :], transfer_ref[p + k, 64:128, :]
            gr, gi = transfer_ref[p + k, 128:192, :], transfer_ref[p + k, 192:256, :]
            if adjoint:
                real = (a * fr + b * fi) - (c * gr + d * gi)
                imag = (b * fr - a * fi) - (d * gr - c * gi)
            else:
                real = (a * fr - b * fi) + (c * gr - d * gi)
                imag = (b * fr + a * fi) + (d * gr + c * gi)
            weighted.append(jnp.concatenate([real, imag], 0))
        result = along_columns(column_back_ref[...], jnp.concatenate(weighted, 1))
        back[p] = result[:, :128]
        back[p + 1] = result[:, 128:]

    def chunk_back(c, carry):
        here = pl.ds(pl.multiple_of(c * 8, 8), 8)
        there = pl.ds(pl.multiple_of(c * 8 + 32, 8), 8)

        def load(plane):
            return back[plane, here, :], back[plane, there, :]

        def store(x, value):
            field[x - 16, here, :] = value

        rows_inverse(load, store)
        return carry

    lax.fori_loop(0, 4, chunk_back, 0)

    matrix = depth_back_ref[...]
    for x in range(0, 32, 16):
        values = field[x : 16 + x].reshape(512, 128)
        result = along_depth(values, matrix).reshape(16, 32, 128)
        if adjoint:
            out_refs[0][x : x + 16] = other_ref[x : x + 16] * result
        else:
            quotient = other_ref[x : x + 16] / result
            out_refs[x // 16][...] = quotient
            if x == 0:
                out_refs[2][...] = quotient[:15]


def vmem(count):
    return [pl.BlockSpec(memory_space=pltpu.VMEM)] * count


def transfer_function(psf, depth):
    size = psf.shape[0]
    offsets = np.arange(size) - size // 2
    return pl.pallas_call(
        transfer_kernel,
        out_shape=jax.ShapeDtypeStruct((PLANES, 256, depth), jnp.float32),
        out_specs=vmem(1)[0],
        scratch_shapes=[
            pltpu.VMEM((size, size, depth), jnp.float32),
            pltpu.VMEM((PLANES, 2 * size, depth), jnp.float32),
        ],
        compiler_params=pltpu.CompilerParams(vmem_limit_bytes=8 * 2**20),
        name="transfer",
    )(
        psf,
        jnp.asarray(depth_forward(offsets, depth), jnp.float32),
        left_operand(column_forward(offsets)),
    )


def edge(side, first, last, above, below):
    return pl.pallas_call(
        functools.partial(edge_kernel, side),
        out_shape=jax.ShapeDtypeStruct((WINDOW, 16, first.shape[2]), jnp.float32),
        in_specs=vmem(4),
        out_specs=vmem(1)[0],
        compiler_params=pltpu.CompilerParams(vmem_limit_bytes=2**20),
        name="edge",
    )(first, last, above, below)


def split(block):
    shape = jax.ShapeDtypeStruct((16,) + block.shape[1:], jnp.float32)
    return pl.pallas_call(
        split_kernel,
        out_shape=(shape, shape),
        in_specs=[pl.BlockSpec(memory_space=pltpu.HBM)],
        out_specs=tuple(vmem(2)),
        scratch_shapes=[pltpu.SemaphoreType.DMA((2,))],
        compiler_params=pltpu.CompilerParams(vmem_limit_bytes=2**20),
        name="split",
    )(block)


def columns(pieces, depth_matrix, name):
    _, width, depth = pieces[0].shape
    return pl.pallas_call(
        functools.partial(columns_kernel, len(pieces)),
        out_shape=jax.ShapeDtypeStruct((PLANES, 2 * width, depth), jnp.float32),
        in_specs=vmem(len(pieces) + 1),
        out_specs=vmem(1)[0],
        scratch_shapes=[pltpu.VMEM((WINDOW, width, depth), jnp.float32)],
        compiler_params=pltpu.CompilerParams(vmem_limit_bytes=8 * 2**20),
        name=name,
    )(*pieces, depth_matrix)


def convolve(pieces, transfer, other, adjoint):
    first, last, above, below, left, right = pieces
    depth = other.shape[2]
    positions = np.arange(WINDOW)
    scale = 1.0 / (WINDOW * WINDOW * depth)
    depth_matrix = right_operand(depth_forward(np.arange(depth), depth))
    inner = columns((above, first, last, below), depth_matrix, "inner")
    left = columns((left,), depth_matrix, "left")
    forward = np.concatenate(
        [
            column_forward(positions[16:48]),
            column_forward(positions[:16]),
            column_forward(positions[48:]),
        ],
        1,
    )
    whole = jax.ShapeDtypeStruct(other.shape, jnp.float32)
    parts = [jax.ShapeDtypeStruct((rows,) + other.shape[1:], jnp.float32) for rows in (16, 16, 15)]
    return pl.pallas_call(
        functools.partial(convolve_kernel, adjoint),
        out_shape=whole if adjoint else tuple(parts),
        in_specs=vmem(9),
        out_specs=vmem(1)[0] if adjoint else tuple(vmem(3)),
        scratch_shapes=[
            pltpu.VMEM((WINDOW, 16, depth), jnp.float32),
            pltpu.VMEM((PLANES, 32, depth), jnp.float32),
            pltpu.VMEM((PLANES, 2 * WINDOW, depth), jnp.float32),
            pltpu.VMEM((PLANES, WINDOW, depth), jnp.float32),
            pltpu.VMEM((32, 32, depth), jnp.float32),
        ],
        compiler_params=pltpu.CompilerParams(vmem_limit_bytes=20 * 2**20),
        name="correlate" if adjoint else "convolve",
    )(
        inner,
        left,
        right,
        transfer,
        other,
        depth_matrix,
        left_operand(forward),
        left_operand(column_inverse(positions[16:48])),
        right_operand(depth_inverse(depth) * scale),
    )


def halos(first, last, down):
    def ring(axis, step):
        count = lax.axis_size(axis)
        return [(i, (i + step) % count) for i in range(count)]

    above = lax.ppermute(last, "px", ring("px", 1))
    below = lax.ppermute(down, "px", ring("px", -1))
    left = lax.ppermute(edge(16, first, last, above, below), "py", ring("py", 1))
    right = lax.ppermute(edge(0, first, last, above, below), "py", ring("py", -1))
    return first, last, above, below, left, right


def variation(volume, pieces):
    _, _, above, below, left, right = pieces
    row_count, col_count, _ = volume.shape
    row_whole = row_count * lax.axis_size("px")
    col_whole = col_count * lax.axis_size("py")
    padded = jnp.concatenate(
        [
            left[15:49, 15:],
            jnp.concatenate([above[15:], volume, below[:1]], 0),
            right[15:49, :1],
        ],
        1,
    )
    region = padded[:-1, :-1]
    slope_rows = padded[1:, :-1] - region
    slope_cols = padded[:-1, 1:] - region
    row_global = lax.axis_index("px") * row_count - 1 + jnp.arange(row_count + 1)
    col_global = lax.axis_index("py") * col_count - 1 + jnp.arange(col_count + 1)
    row_valid = ((row_global >= 0) & (row_global <= row_whole - 2))[:, None, None]
    col_valid = ((col_global >= 0) & (col_global <= col_whole - 2))[None, :, None]
    slope_rows = jnp.where(row_valid, slope_rows, 0.0)
    slope_cols = jnp.where(col_valid, slope_cols, 0.0)
    slope_depth = jnp.concatenate(
        [region[:, :, 1:] - region[:, :, :-1], jnp.zeros_like(region[:, :, :1])], 2
    )
    factor = lax.rsqrt(
        slope_rows * slope_rows
        + slope_cols * slope_cols
        + slope_depth * slope_depth
        + smoothing * smoothing
    )
    flux_rows, flux_cols = slope_rows * factor, slope_cols * factor
    flux_depth = (slope_depth * factor)[1:, 1:]
    flux_depth = flux_depth - jnp.concatenate(
        [jnp.zeros_like(flux_depth[:, :, :1]), flux_depth[:, :, :-1]], 2
    )
    return (
        flux_rows[1:, 1:]
        - flux_rows[:-1, 1:]
        + (flux_cols[1:, 1:] - flux_cols[1:, :-1])
        + flux_depth
    )


def shards(estimate, observed, psf):
    transfer = transfer_function(psf, estimate.shape[2])
    first, last = split(estimate)
    pieces = halos(first, last, first)
    quotient = convolve(pieces, transfer, observed, False)
    around, quotient = lax.optimization_barrier((pieces[2:], quotient))
    scaled = estimate / (1.0 - penalty_weight * variation(estimate, pieces[:2] + around))
    return convolve(halos(*quotient), transfer, scaled, True)


def solution(mesh):
    placed = (P("px", "py", None), P("px", "py", None), P())
    return jax.shard_map(
        shards, mesh=mesh, in_specs=placed, out_specs=P("px", "py", None), check_vma=False
    )
```

```python
import functools
import math

import jax
import jax.numpy as jnp
import ml_dtypes
import numpy as np
from jax import lax
from jax.experimental import pallas as pl
from jax.experimental.pallas import tpu as pltpu
from jax.sharding import PartitionSpec as P

penalty_weight = 0.1
smoothing = 0.1

WINDOW = 64
PLANES = 34
ROOT = math.sqrt(0.5)


def two_part(matrix):
    high = matrix.astype(ml_dtypes.bfloat16)
    low = (matrix - high.astype(np.float64)).astype(ml_dtypes.bfloat16)
    return high, low


def right_operand(matrix):
    high, low = two_part(matrix)
    return np.block([[high, low], [high, np.zeros_like(high)]])


def left_operand(matrix):
    high, low = two_part(matrix)
    return np.block([[high, high], [low, np.zeros_like(high)]])


def depth_forward(positions, depth):
    half = depth // 2
    turns = 2.0 * np.pi / depth
    real = np.cos(turns * np.outer(positions, np.arange(half + 1)))
    imag = -np.sin(turns * np.outer(positions, np.arange(1, half)))
    return np.concatenate([real, imag], 1)


def depth_inverse(depth):
    half = depth // 2
    turns = 2.0 * np.pi / depth
    positions = np.arange(depth)
    weight = np.full(half + 1, 2.0)
    weight[0] = weight[half] = 1.0
    real = weight[:, None] * np.cos(turns * np.outer(np.arange(half + 1), positions))
    imag = -2.0 * np.sin(turns * np.outer(np.arange(1, half), positions))
    return np.concatenate([real, imag], 0)


def column_forward(positions):
    angles = 2.0 * np.pi / WINDOW * np.outer(np.arange(WINDOW), positions)
    cosine, sine = np.cos(angles), np.sin(angles)
    return np.block([[cosine, sine], [-sine, cosine]])


def column_inverse(positions):
    angles = 2.0 * np.pi / WINDOW * np.outer(positions, np.arange(WINDOW))
    cosine, sine = np.cos(angles), np.sin(angles)
    return np.block([[cosine, -sine], [sine, cosine]])


def add(a, b):
    return (a[0] + b[0], a[1] + b[1])


def sub(a, b):
    return (a[0] - b[0], a[1] - b[1])


def turn(a, eighths):
    real, imag = a
    eighths %= 8
    if eighths == 0:
        return a
    if eighths == 2:
        return (-imag, real)
    if eighths == 4:
        return (-real, -imag)
    if eighths == 6:
        return (imag, -real)
    total, gap = (real + imag) * ROOT, (real - imag) * ROOT
    if eighths == 1:
        return (gap, total)
    if eighths == 3:
        return (-total, gap)
    if eighths == 5:
        return (-gap, -total)
    return (total, -gap)


def twiddle(a, power, sign):
    angle = sign * 2.0 * math.pi * power / WINDOW
    cosine, sine = math.cos(angle), math.sin(angle)
    if power == 0:
        return a
    real, imag = a
    return (real * cosine - imag * sine, real * sine + imag * cosine)


def complex_eight(values, sign):
    if len(values) == 1:
        return values
    count = len(values)
    even = complex_eight(values[0::2], sign)
    odd = complex_eight(values[1::2], sign)
    odd = [turn(value, sign * k * (8 // count)) for k, value in enumerate(odd)]
    return [add(e, o) for e, o in zip(even, odd)] + [sub(e, o) for e, o in zip(even, odd)]


def real_eight(a):
    s04, d04, s26, d26 = a[0] + a[4], a[0] - a[4], a[2] + a[6], a[2] - a[6]
    s15, d15, s37, d37 = a[1] + a[5], a[1] - a[5], a[3] + a[7], a[3] - a[7]
    even, odd = s04 + s26, s15 + s37
    gap, total = (d15 - d37) * ROOT, (d15 + d37) * ROOT
    return (
        even + odd,
        (d04 + gap, -d26 - total),
        (s04 - s26, s37 - s15),
        (d04 - gap, d26 - total),
        even - odd,
    )


def rows_forward(load, store, zero):
    first = [real_eight([load(8 * x1 + x0) for x1 in range(8)]) for x0 in range(8)]
    ends = real_eight([f[0] for f in first])
    store(0, ends[0], zero)
    for k0 in (1, 2, 3):
        store(k0, *ends[k0])
    store(4, ends[4], zero)
    plane = 5
    for k1 in (1, 2, 3):
        out = complex_eight([twiddle(first[x0][k1], k1 * x0, -1) for x0 in range(8)], -1)
        for value in out:
            store(plane, *value)
            plane += 1
    middle = []
    for x0 in range(8):
        angle = 2.0 * math.pi * 4 * x0 / WINDOW
        middle.append((first[x0][4] * math.cos(angle), first[x0][4] * -math.sin(angle)))
    middle = complex_eight(middle, -1)
    for k0 in range(4):
        store(plane, *middle[k0])
        plane += 1


def rows_inverse(load, store):
    ends = [load(p) for p in range(5)]
    x0r, x4r = ends[0][0], ends[4][0]
    spectrum = [(x0r, jnp.zeros_like(x0r))] + [ends[k] for k in (1, 2, 3)]
    parts = [[None] * 8 for _ in range(5)]
    (r1, i1), (r2, i2), (r3, i3) = [(2.0 * e[0], 2.0 * e[1]) for e in ends[1:4]]
    del spectrum
    base, flip = x0r + x4r, x0r - x4r
    g13, t13 = r1 - r3, r1 + r3
    h13, u13 = i1 - i3, i1 + i3
    parts[0][0] = base + t13 + r2
    parts[0][4] = base - t13 + r2
    parts[0][2] = base - r2 - h13
    parts[0][6] = base - r2 + h13
    odd_a, odd_b = g13 * ROOT, u13 * ROOT
    parts[0][1] = flip + odd_a - odd_b - i2
    parts[0][5] = flip - odd_a + odd_b - i2
    parts[0][3] = flip - odd_a - odd_b + i2
    parts[0][7] = flip + odd_a + odd_b + i2
    plane = 5
    for k1 in (1, 2, 3):
        values = complex_eight([load(plane + k0) for k0 in range(8)], 1)
        plane += 8
        parts[k1] = [twiddle(values[x0], k1 * x0, 1) for x0 in range(8)]
    half = [load(plane + k0) for k0 in range(4)]
    middle = complex_eight(half + [(half[3 - k][0], -half[3 - k][1]) for k in range(4)], 1)
    for x0 in range(8):
        angle = 2.0 * math.pi * 4 * x0 / WINDOW
        parts[4][x0] = middle[x0][0] * math.cos(angle) - middle[x0][1] * math.sin(angle)
    for x0 in range(8):
        v0, v4 = parts[0][x0], parts[4][x0]
        (a, b), (c, d), (e, f) = parts[1][x0], parts[2][x0], parts[3][x0]
        plus, minus = v0 + v4, v0 - v4
        store(16 + x0, plus + 2.0 * (f - b - c))
        store(24 + x0, minus + 2.0 * (d + ROOT * ((e - f) - (a + b))))
        store(32 + x0, plus + 2.0 * (c - a - e))
        store(40 + x0, minus + 2.0 * (ROOT * ((b - a) + (e + f)) - d))


def parts_of(value):
    high = value.astype(jnp.bfloat16)
    low = (value - high.astype(jnp.float32)).astype(jnp.bfloat16)
    return high, low


def along_depth(rows, matrix):
    high, low = parts_of(rows)
    out = jnp.dot(
        jnp.concatenate([high, low], 1), matrix, preferred_element_type=jnp.float32
    )
    return out[:, :128] + out[:, 128:]


def along_columns(matrix, value):
    high, low = parts_of(value)
    out = jnp.dot(
        matrix, jnp.concatenate([high, low], 0), preferred_element_type=jnp.float32
    )
    half = out.shape[0] // 2
    return out[:half] + out[half:]


def transfer_kernel(psf_ref, depth_ref, column_ref, factors, field, rows):
    size = psf_ref.shape[0]
    for x in range(0, size, 8):
        values = psf_ref[x : x + 8].reshape(8 * size, size)
        field[x : x + 8] = jnp.dot(
            values,
            depth_ref[...],
            precision=lax.Precision.HIGHEST,
            preferred_element_type=jnp.float32,
        ).reshape(8, size, 128)
    zero = jnp.zeros((8, 128), jnp.float32)
    rows[PLANES - 1] = jnp.zeros_like(rows[0])

    def chunk(c, carry):
        here = pl.ds(pl.multiple_of(c * 8, 8), 8)
        there = pl.ds(pl.multiple_of(c * 8 + size, 8), 8)

        def load(x):
            tap = (x + size // 2) % WINDOW
            return field[tap, here, :] if tap < size else zero

        def store(plane, real, imag):
            rows[plane, here, :] = real
            rows[plane, there, :] = imag

        rows_forward(load, store, zero)
        return carry

    lax.fori_loop(0, size // 8, chunk, 0)
    lane = lax.broadcasted_iota(jnp.int32, (1, 128), 1)
    real_lane = lane <= 64
    first_half = lane < 64
    alone = (lane == 0) | (lane == 64)
    for p in range(0, PLANES, 2):
        both = along_columns(column_ref[...], jnp.concatenate([rows[p], rows[p + 1]], 1))
        for k in range(2):
            spectrum = both[:, 128 * k : 128 * (k + 1)]
            other = pltpu.roll(spectrum, 64, 1)
            factors[p + k, :128, :] = jnp.where(real_lane, spectrum, other)
            factors[p + k, 128:, :] = jnp.where(
                alone, 0.0, jnp.where(first_half, -other, spectrum)
            )


def depth_piece(ref, matrix, field, x_from, y_from):
    count, width, lanes = ref.shape
    step = 512 // width
    for x in range(0, count, step):
        size = min(step, count - x)
        values = ref[x : x + size].reshape(size * width, lanes)
        field[x_from + x : x_from + x + size, y_from : y_from + width, :] = along_depth(
            values, matrix
        ).reshape(size, width, lanes)


def row_transforms(field, rows, width):
    zero = jnp.zeros((8, 128), jnp.float32)
    rows[PLANES - 1] = jnp.zeros_like(rows[0])

    def chunk(c, carry):
        here = pl.ds(pl.multiple_of(c * 8, 8), 8)
        there = pl.ds(pl.multiple_of(c * 8 + width, 8), 8)

        def load(x):
            return field[x, here, :]

        def store(plane, real, imag):
            rows[plane, here, :] = real
            rows[plane, there, :] = imag

        rows_forward(load, store, zero)
        return carry

    lax.fori_loop(0, width // 8, chunk, 0, unroll=2)


def edge_kernel(side, first_ref, last_ref, above_ref, below_ref, out_ref):
    at = 0
    for ref in (above_ref, first_ref, last_ref, below_ref):
        count = ref.shape[0]
        out_ref[at : at + count] = ref[:, side : side + 16, :]
        at += count
    if at < WINDOW:
        out_ref[at] = jnp.zeros_like(out_ref[0])


def split_kernel(block_ref, first_ref, last_ref, done):
    copies = [
        pltpu.make_async_copy(block_ref.at[pl.ds(16 * i, 16)], ref, done.at[i])
        for i, ref in enumerate((first_ref, last_ref))
    ]
    for copy in copies:
        copy.start()
    for copy in copies:
        copy.wait()


def columns_kernel(count, *refs):
    pieces, (depth_ref, rows_ref, field) = refs[:count], refs[count:]
    matrix = depth_ref[...]
    at = 0
    for ref in pieces:
        depth_piece(ref, matrix, field, at, 0)
        at += ref.shape[0]
    if at < WINDOW:
        field[at] = jnp.zeros_like(field[0])
    row_transforms(field, rows_ref, field.shape[1])


def convolve_kernel(
    adjoint,
    inner_ref,
    left_ref,
    right_ref,
    transfer_ref,
    other_ref,
    depth_ref,
    column_ref,
    column_back_ref,
    depth_back_ref,
    *out_refs_and_scratch,
):
    *out_refs, right_field, rows, spectra, back, field = out_refs_and_scratch
    depth_piece(right_ref, depth_ref[...], right_field, 0, 0)
    row_transforms(right_field, rows, 16)

    for p in range(0, PLANES, 2):
        spectrum = along_columns(
            column_ref[...],
            jnp.concatenate(
                [
                    jnp.concatenate([inner_ref[k], left_ref[k], rows[k]], 0)
                    for k in (p, p + 1)
                ],
                1,
            ),
        )
        spectra[p] = spectrum[:, :128]
        spectra[p + 1] = spectrum[:, 128:]

    for p in range(0, PLANES, 2):
        weighted = []
        for k in range(2):
            own = spectra[p + k]
            partner = pltpu.roll(own, 64, 1)
            a, b = own[:64], own[64:]
            c, d = partner[:64], partner[64:]
            fr, fi = transfer_ref[p + k, 0:64, :], transfer_ref[p + k, 64:128, :]
            gr, gi = transfer_ref[p + k, 128:192, :], transfer_ref[p + k, 192:256, :]
            if adjoint:
                real = (a * fr + b * fi) - (c * gr + d * gi)
                imag = (b * fr - a * fi) - (d * gr - c * gi)
            else:
                real = (a * fr - b * fi) + (c * gr - d * gi)
                imag = (b * fr + a * fi) + (d * gr + c * gi)
            weighted.append(jnp.concatenate([real, imag], 0))
        result = along_columns(column_back_ref[...], jnp.concatenate(weighted, 1))
        back[p] = result[:, :128]
        back[p + 1] = result[:, 128:]

    def chunk_back(c, carry):
        here = pl.ds(pl.multiple_of(c * 8, 8), 8)
        there = pl.ds(pl.multiple_of(c * 8 + 32, 8), 8)

        def load(plane):
            return back[plane, here, :], back[plane, there, :]

        def store(x, value):
            field[x - 16, here, :] = value

        rows_inverse(load, store)
        return carry

    lax.fori_loop(0, 4, chunk_back, 0, unroll=2)

    matrix = depth_back_ref[...]
    for x in range(0, 32, 16):
        values = field[x : 16 + x].reshape(512, 128)
        result = along_depth(values, matrix).reshape(16, 32, 128)
        if adjoint:
            out_refs[0][x : x + 16] = other_ref[x : x + 16] * result
        else:
            quotient = other_ref[x : x + 16] / result
            out_refs[x // 16][...] = quotient
            if x == 0:
                out_refs[2][...] = quotient[:15]


def vmem(count):
    return [pl.BlockSpec(memory_space=pltpu.VMEM)] * count


def transfer_function(psf, depth):
    size = psf.shape[0]
    offsets = np.arange(size) - size // 2
    return pl.pallas_call(
        transfer_kernel,
        out_shape=jax.ShapeDtypeStruct((PLANES, 256, depth), jnp.float32),
        out_specs=vmem(1)[0],
        scratch_shapes=[
            pltpu.VMEM((size, size, depth), jnp.float32),
            pltpu.VMEM((PLANES, 2 * size, depth), jnp.float32),
        ],
        compiler_params=pltpu.CompilerParams(vmem_limit_bytes=8 * 2**20),
        name="transfer",
    )(
        psf,
        jnp.asarray(depth_forward(offsets, depth), jnp.float32),
        left_operand(column_forward(offsets)),
    )


def edge(side, first, last, above, below):
    return pl.pallas_call(
        functools.partial(edge_kernel, side),
        out_shape=jax.ShapeDtypeStruct((WINDOW, 16, first.shape[2]), jnp.float32),
        in_specs=vmem(4),
        out_specs=vmem(1)[0],
        compiler_params=pltpu.CompilerParams(vmem_limit_bytes=2**20),
        name="edge",
    )(first, last, above, below)


def split(block):
    shape = jax.ShapeDtypeStruct((16,) + block.shape[1:], jnp.float32)
    return pl.pallas_call(
        split_kernel,
        out_shape=(shape, shape),
        in_specs=[pl.BlockSpec(memory_space=pltpu.HBM)],
        out_specs=tuple(vmem(2)),
        scratch_shapes=[pltpu.SemaphoreType.DMA((2,))],
        compiler_params=pltpu.CompilerParams(vmem_limit_bytes=2**20),
        name="split",
    )(block)


def columns(pieces, depth_matrix, name):
    _, width, depth = pieces[0].shape
    return pl.pallas_call(
        functools.partial(columns_kernel, len(pieces)),
        out_shape=jax.ShapeDtypeStruct((PLANES, 2 * width, depth), jnp.float32),
        in_specs=vmem(len(pieces) + 1),
        out_specs=vmem(1)[0],
        scratch_shapes=[pltpu.VMEM((WINDOW, width, depth), jnp.float32)],
        compiler_params=pltpu.CompilerParams(vmem_limit_bytes=8 * 2**20),
        name=name,
    )(*pieces, depth_matrix)


def convolve(pieces, transfer, other, adjoint):
    first, last, above, below, left, right = pieces
    depth = other.shape[2]
    positions = np.arange(WINDOW)
    scale = 1.0 / (WINDOW * WINDOW * depth)
    depth_matrix = right_operand(depth_forward(np.arange(depth), depth))
    inner = columns((above, first, last, below), depth_matrix, "inner")
    left = columns((left,), depth_matrix, "left")
    forward = np.concatenate(
        [
            column_forward(positions[16:48]),
            column_forward(positions[:16]),
            column_forward(positions[48:]),
        ],
        1,
    )
    whole = jax.ShapeDtypeStruct(other.shape, jnp.float32)
    parts = [jax.ShapeDtypeStruct((rows,) + other.shape[1:], jnp.float32) for rows in (16, 16, 15)]
    return pl.pallas_call(
        functools.partial(convolve_kernel, adjoint),
        out_shape=whole if adjoint else tuple(parts),
        in_specs=vmem(9),
        out_specs=vmem(1)[0] if adjoint else tuple(vmem(3)),
        scratch_shapes=[
            pltpu.VMEM((WINDOW, 16, depth), jnp.float32),
            pltpu.VMEM((PLANES, 32, depth), jnp.float32),
            pltpu.VMEM((PLANES, 2 * WINDOW, depth), jnp.float32),
            pltpu.VMEM((PLANES, WINDOW, depth), jnp.float32),
            pltpu.VMEM((32, 32, depth), jnp.float32),
        ],
        compiler_params=pltpu.CompilerParams(vmem_limit_bytes=20 * 2**20),
        name="correlate" if adjoint else "convolve",
    )(
        inner,
        left,
        right,
        transfer,
        other,
        depth_matrix,
        left_operand(forward),
        left_operand(column_inverse(positions[16:48])),
        right_operand(depth_inverse(depth) * scale),
    )


def halos(first, last, down):
    def ring(axis, step):
        count = lax.axis_size(axis)
        return [(i, (i + step) % count) for i in range(count)]

    above = lax.ppermute(last, "px", ring("px", 1))
    below = lax.ppermute(down, "px", ring("px", -1))
    left = lax.ppermute(edge(16, first, last, above, below), "py", ring("py", 1))
    right = lax.ppermute(edge(0, first, last, above, below), "py", ring("py", -1))
    return first, last, above, below, left, right


def variation(volume, pieces):
    _, _, above, below, left, right = pieces
    row_count, col_count, _ = volume.shape
    row_whole = row_count * lax.axis_size("px")
    col_whole = col_count * lax.axis_size("py")
    padded = jnp.concatenate(
        [
            left[15:49, 15:],
            jnp.concatenate([above[15:], volume, below[:1]], 0),
            right[15:49, :1],
        ],
        1,
    )
    region = padded[:-1, :-1]
    slope_rows = padded[1:, :-1] - region
    slope_cols = padded[:-1, 1:] - region
    row_global = lax.axis_index("px") * row_count - 1 + jnp.arange(row_count + 1)
    col_global = lax.axis_index("py") * col_count - 1 + jnp.arange(col_count + 1)
    row_valid = ((row_global >= 0) & (row_global <= row_whole - 2))[:, None, None]
    col_valid = ((col_global >= 0) & (col_global <= col_whole - 2))[None, :, None]
    slope_rows = jnp.where(row_valid, slope_rows, 0.0)
    slope_cols = jnp.where(col_valid, slope_cols, 0.0)
    slope_depth = jnp.concatenate(
        [region[:, :, 1:] - region[:, :, :-1], jnp.zeros_like(region[:, :, :1])], 2
    )
    factor = lax.rsqrt(
        slope_rows * slope_rows
        + slope_cols * slope_cols
        + slope_depth * slope_depth
        + smoothing * smoothing
    )
    flux_rows, flux_cols = slope_rows * factor, slope_cols * factor
    flux_depth = (slope_depth * factor)[1:, 1:]
    flux_depth = flux_depth - jnp.concatenate(
        [jnp.zeros_like(flux_depth[:, :, :1]), flux_depth[:, :, :-1]], 2
    )
    return (
        flux_rows[1:, 1:]
        - flux_rows[:-1, 1:]
        + (flux_cols[1:, 1:] - flux_cols[1:, :-1])
        + flux_depth
    )


def shards(estimate, observed, psf):
    transfer = transfer_function(psf, estimate.shape[2])
    first, last = split(estimate)
    pieces = halos(first, last, first)
    quotient = convolve(pieces, transfer, observed, False)
    around, quotient = lax.optimization_barrier((pieces[2:], quotient))
    scaled = estimate / (1.0 - penalty_weight * variation(estimate, pieces[:2] + around))
    return convolve(halos(*quotient), transfer, scaled, True)


def solution(mesh):
    placed = (P("px", "py", None), P("px", "py", None), P())
    return jax.shard_map(
        shards, mesh=mesh, in_specs=placed, out_specs=P("px", "py", None), check_vma=False
    )
```
